32 devices in a mesh: row: 8 (over z, core), col: 4 (over y, x).
Axes of the slice: x: 2, y: 2, z: 4, core: 2. Of those that a mesh axis runs over, the one named last changes fastest.
Arguments:
- covariance: float32 [8192, 8192], P('row', 'col'), as said below
- state_mean: float32 [8192], P('row'), may hold values from -6 to 6
- obs_values: float32 [2, 256], replicated, may hold values from -8 to 8
- obs_cells: int32 [2, 4, 256], replicated, may hold values from 0 to 8191
- obs_weights: float32 [2, 4, 256], replicated, may hold values from 0.2 to 1
- obs_variance: float32 [2, 256], replicated, may hold values from 0.05 to 1
Outputs:
- covariance_after: float32 [8192, 8192], P('row', 'col')
- state_after: float32 [8192], P('row')
The draws below stay inside these ranges and needn't reach their ends.
Inputs may be any that keep to these rules, and one draw needn't show every extreme that they name: `covariance`: symmetric and positive definite.
All inputs are finite; a program needn't handle non-finite values.
Results may differ from the reference program's by a relative error of at most 0.0001.
Values sent between devices are 32-bit elements; how exact they have to be, the bound alone decides.
A program may use at most 64 MiB of HBM per device.

```python
import math
import jax
import jax.numpy as jnp
from jax import lax

STATE = 8192
OBS = 256
FOOT = 4
BATCHES = 2


def draw_covariance(key, part):
    noise = jax.random.normal(jax.random.fold_in(key, 11), (STATE, STATE), jnp.float32)
    sym = (noise + noise.T) * (0.35 / math.sqrt(STATE))
    diag = jax.random.uniform(jax.random.fold_in(key, 12), (STATE,), jnp.float32, 1.5, 2.5)
    matrix = sym + jnp.diag(diag)
    return matrix


def place_ends(drawn, own_key, least, high):
    shape = drawn.shape
    spot = [jax.random.randint(jax.random.fold_in(own_key, axis), (), 0, shape[axis]) for axis in range(len(shape))]
    drawn = drawn.at[tuple(spot)].set(least)
    longest = shape.index(max(shape))
    spot[longest] = (spot[longest] + 1) % shape[longest]
    return drawn.at[tuple(spot)].set(high)


def block_levels(key, shape, split, smallest, top_value):
    level, own = 1.0, jax.random.fold_in(key, 6)
    for position, blocks in split:
        steps = jnp.exp(jax.random.uniform(jax.random.fold_in(own, position), (blocks,), jnp.float32, smallest / len(split), top_value / len(split)))
        level = level * jnp.repeat(steps, shape[position] // blocks).reshape([-1 if axis == position else 1 for axis in range(len(shape))])
    return level


def bell_draw(rng, shape, scale, limit, shards=(), kind=jnp.bfloat16):
    array = jax.random.normal(rng, shape, jnp.float32) * scale
    if len(shards) > 0:
        array = block_levels(rng, shape, shards, -0.22, 0.18) * array
    return jnp.clip(array, min=-limit, max=limit).astype(kind)


def setup_inputs(seed: int = 0) -> dict:
    seeds = jax.random.split(jax.random.key(seed), 7)
    covariance = draw_covariance(jax.random.fold_in(seeds[6], 71), 0)
    state_mean = bell_draw(seeds[1], (STATE,), 1.0, 6.0, ((0, 8),), jnp.float32)
    obs_values = bell_draw(seeds[2], (BATCHES, OBS), 2.0, 8.0, (), jnp.float32)
    obs_cells = place_ends(jax.random.randint(seeds[3], (BATCHES, FOOT, OBS), 0, STATE), jax.random.fold_in(seeds[3], 1), 0, STATE - 1).astype(jnp.int32)
    obs_weights = jnp.clip(jax.random.uniform(seeds[4], (BATCHES, FOOT, OBS), jnp.float32, 0.2, 1.0), 0.2, 1.0)
    obs_variance = jnp.clip(jnp.exp(jax.random.uniform(seeds[5], (BATCHES, OBS), jnp.float32, math.log(0.05), math.log(1.0))), 0.05, 1.0)
    return {"covariance": covariance, "state_mean": state_mean, "obs_values": obs_values, "obs_cells": obs_cells, "obs_weights": obs_weights, "obs_variance": obs_variance}


def reference(covariance, state_mean, obs_values, obs_cells, obs_weights, obs_variance):
    hi = lax.Precision.HIGHEST
    matrix = covariance
    mean = state_mean
    for batch in range(BATCHES):
        cells = obs_cells[batch]
        weights = obs_weights[batch]
        cross = jnp.zeros((STATE, OBS), jnp.float32)
        for foot in range(FOOT):
            cross = cross + matrix[:, cells[foot]] * weights[foot][None, :]
        inner = jnp.zeros((OBS, OBS), jnp.float32)
        predicted = jnp.zeros((OBS,), jnp.float32)
        for foot in range(FOOT):
            inner = inner + weights[foot][:, None] * cross[cells[foot], :]
            predicted = predicted + weights[foot] * mean[cells[foot]]
        inner = 0.5 * (inner + inner.T) + jnp.diag(obs_variance[batch])
        factor = jnp.linalg.cholesky(inner)
        gain = lax.linalg.triangular_solve(factor, cross.T, left_side=True, lower=True).T
        innov = (obs_values[batch] - predicted)[:, None]
        white = lax.linalg.triangular_solve(factor, innov, left_side=True, lower=True)[:, 0]
        mean = mean + jnp.dot(gain.astype(jnp.float32), white.astype(jnp.float32), precision=hi, preferred_element_type=jnp.float32)
        matrix = matrix - jnp.dot(gain.astype(jnp.float32), gain.T.astype(jnp.float32), precision=hi, preferred_element_type=jnp.float32)
    return (matrix, mean)
```

```python
import functools

import jax
import jax.numpy as jnp
from jax import lax
from jax.experimental import pallas as pl
from jax.experimental.pallas import tpu as pltpu
from jax.sharding import PartitionSpec as P

HI = lax.Precision.HIGHEST
MID = lax.Precision.HIGH
MESH = pl.DeviceIdType.MESH
BLK = 128
SUB = 8

def base_inverse(work, hook):
    def panel_step(first, g, carry):
        start = pl.multiple_of(g * SUB, SUB)
        panel = work[pl.ds(start, SUB), :]
        square = pltpu.roll(panel[:, :BLK], BLK - start, 1)[:, :SUB]
        wide = [jnp.broadcast_to(square[:, j : j + 1], (SUB, BLK)) for j in range(SUB)]
        left, right = panel[:, :BLK], panel[:, BLK:]
        below = lax.broadcasted_iota(jnp.int32, (SUB, BLK), 0)
        scale = jnp.zeros((SUB, BLK), jnp.float32)
        for j in range(SUB):
            pivot = jnp.broadcast_to(wide[j][j : j + 1, :], (SUB, BLK))
            inv = 1.0 / pivot
            scale = jnp.where(below == j, lax.rsqrt(pivot), scale)
            ratio = jnp.where(below > j, wide[j] * inv, 0.0)
            left = left - ratio * left[j : j + 1, :]
            right = right - ratio * right[j : j + 1, :]
            for k in range(j + 1, SUB):
                wide[k] = wide[k] - ratio * wide[k][j : j + 1, :]
        left = left * scale
        right = right * scale
        both = jnp.concatenate([left, right], axis=1)
        lane = lax.broadcasted_iota(jnp.int32, (SUB, BLK), 1)
        lhs = jnp.where(lane >= start + SUB, left, 0.0)
        work[pl.ds(start, SUB), :] = both
        work[first:, :] = work[first:, :] - lax.dot_general(lhs[:, first:], both, (((0,), (0,)), ((), ())), precision=HI, preferred_element_type=jnp.float32)
        return carry
    steps = BLK // SUB // 4
    for quarter in range(4):
        hook(quarter)
        first = quarter * steps * SUB
        lax.fori_loop(quarter * steps, (quarter + 1) * steps, functools.partial(panel_step, first), 0)

def factor_inverse(mat, work, hook):
    size = mat.shape[0]
    eye = (lax.broadcasted_iota(jnp.int32, (BLK, BLK), 0) == lax.broadcasted_iota(jnp.int32, (BLK, BLK), 1)).astype(jnp.float32)
    for b in range(size // BLK):
        lo, hi = b * BLK, (b + 1) * BLK
        work[:, :BLK] = mat[lo:hi, lo:hi]
        work[:, BLK:] = eye
        base_inverse(work, lambda quarter: hook(4 * b + quarter))
        winv = work[:, BLK:]
        if hi < size:
            panel = jnp.dot(winv, mat[lo:hi, hi:size], precision=HI, preferred_element_type=jnp.float32)
        if lo > 0:
            left = jnp.dot(winv, mat[lo:hi, size : size + lo], precision=HI, preferred_element_type=jnp.float32)
            mat[lo:hi, size : size + lo] = left
        mat[lo:hi, size + lo : size + hi] = winv
        if hi < size:
            right = mat[lo:hi, size : size + hi]
            dims = (((0,), (0,)), ((), ()))
            mat[hi:size, hi:size] = mat[hi:size, hi:size] - lax.dot_general(panel, panel, dims, precision=HI, preferred_element_type=jnp.float32)
            mat[hi:size, size : size + hi] = mat[hi:size, size : size + hi] - lax.dot_general(panel, right, dims, precision=HI, preferred_element_type=jnp.float32)


def pair_blocks(size):
    count = size // BLK
    return [(i, j) for i in range(count) for j in range(i + 1)]


def split(value):
    high = value.astype(jnp.bfloat16)
    return high, (value - high.astype(jnp.float32)).astype(jnp.bfloat16)


def matmul(a, b, dims=(((1,), (0,)), ((), ()))):
    return lax.dot_general(a, b, dims, preferred_element_type=jnp.float32)


def part_count(rows, nc):
    return 4 if rows % (4 * nc * SUB) == 0 else 2


def relay_order(nc, parts):
    order = []
    for pair in range(0, parts, 2):
        order += [(0, pair), (0, pair + 1)]
        order += [(d, h) for h in (pair, pair + 1) for d in range(1, nc)]
    return order


def kernel(
    nr, nc, parts, p_ref, x_ref, cells_ref, weights_ref, var_ref, u_ref, xc_ref, pred_ref,
    block, high_op, low_op, row_op, t_ref, xr_ref, acc, full, land, tland, mat, work, send_sem, recv_sem, load_sem,
):
    ratio = nr // nc
    row, col = lax.axis_index("row"), lax.axis_index("col")
    high, low = row // ratio, row % ratio
    packed = acc.shape[0]
    rows, size = t_ref.shape
    wide = block.shape[1]
    part = rows // parts
    sub = part // nc
    order = relay_order(nc, parts)
    pieces = len(order)
    used = [0]

    def take(count):
        used[0] += count
        return used[0] - count

    loads = []
    for h in range(parts):
        where = pl.ds(h * part, part)
        loads.append(pltpu.make_async_copy(p_ref.at[where], block.at[where], load_sem.at[h]))
        loads[-1].start()

    levels = [
        (ratio, low, lambda d: (high * ratio + lax.rem(low + d, ratio), col)),
        (nc, col, lambda d: (row, lax.rem(col + d, nc))),
        (nc, high, lambda d: (lax.rem(high + d, nc) * ratio + low, col)),
    ]
    barrier = pltpu.get_barrier_semaphore()
    for n, me, peer in levels:
        for d in range(1, n):
            pl.semaphore_signal(barrier, inc=1, device_id=peer(d), device_id_type=MESH)

    def operator(first, count, store):
        step = min(count, BLK)
        batches, foot, width = cells_ref.shape

        def fill(g, carry):
            start = pl.multiple_of(g * step, step)
            place = lax.broadcasted_iota(jnp.int32, (step, width), 0) + (first + start)
            for b in range(batches):
                total = jnp.zeros((step, width), jnp.float32)
                for f in range(foot):
                    total = total + jnp.where(cells_ref[b, f : f + 1, :] == place, weights_ref[b, f : f + 1, :], 0.0)
                store(start, step, b * width, width, total)
            return carry

        lax.fori_loop(0, count // step, fill, 0)

    def store_col(start, step, lane, width, total):
        h, l = split(total)
        high_op[pl.ds(start, step), lane : lane + width] = h
        low_op[pl.ds(start, step), lane : lane + width] = l

    def store_row(start, step, lane, width, total):
        row_op[pl.ds(start, step), lane : lane + width] = total

    operator(col * wide, wide, store_col)

    def remote(src, dst, sem, device):
        return pltpu.make_async_remote_copy(
            src_ref=src, dst_ref=dst, send_sem=send_sem.at[sem], recv_sem=recv_sem.at[sem],
            device_id=device, device_id_type=MESH,
        )

    def own_rows(h, owner):
        return pl.ds(pl.multiple_of(h * part + owner * sub, 8), sub)

    _, _, col_peer = levels[1]
    _, _, low_peer = levels[0]
    t_base = take(parts * (nc - 1))
    gather_base = take(parts * (nc - 1))
    chain_base = take(pieces)
    down_base = take(pieces)
    sib_base = take(pieces * (ratio - 1))
    t_copies, gathers = [], []
    for h in range(parts):
        t_copies.append([])
        gathers.append([])
        for d in range(1, nc):
            src = t_ref.at[own_rows(h, lax.rem(col + d, nc))]
            dst = tland.at[d - 1, pl.ds(h * sub, sub)]
            t_copies[h].append(remote(src, dst, t_base + h * (nc - 1) + d - 1, col_peer(d)))
            own = xr_ref.at[own_rows(h, col)]
            gathers[h].append(remote(own, own, gather_base + h * (nc - 1) + d - 1, col_peer(d)))

    def start_all(copies):
        for copy in copies:
            copy.start()

    source = high == col
    far = jnp.abs(high - col)
    top = nc - 1
    above = (jnp.minimum(high + 1, top) * ratio + low, col)
    below = (jnp.maximum(high - 1, 0) * ratio + low, col)
    goes_up = jnp.logical_and(high >= col, high < top)
    goes_down = jnp.logical_and(high <= col, high > 0)

    def links(e, src_is_own):
        d, h = order[e]
        where = own_rows(h, lax.rem(col - d + nc, nc))
        dst = xc_ref.at[low, where]
        src = xr_ref.at[where] if src_is_own else dst
        up = remote(src, dst, chain_base + e, above)
        down = pltpu.make_async_remote_copy(
            src_ref=src, dst_ref=dst, send_sem=send_sem.at[down_base + e],
            recv_sem=recv_sem.at[chain_base + e], device_id=below, device_id_type=MESH,
        )
        sibs = [remote(src, dst, sib_base + e * (ratio - 1) + q - 1, low_peer(q)) for q in range(1, ratio)]
        return where, up, down, sibs

    def send_on(up, down, sibs):
        @pl.when(goes_up)
        def _():
            up.start()

        @pl.when(goes_down)
        def _():
            down.start()

        for sib in sibs:
            sib.start()

    def relay_source(e):
        d, h = order[e]
        if d > 0:
            gathers[h][d - 1].wait_recv()
        where, up, down, sibs = links(e, True)
        send_on(up, down, sibs)
        xc_ref[low, where, :] = xr_ref[where, :]

    def relay(e):
        where, up, down, sibs = links(e, False)
        up.wait_recv()
        send_on(up, down, sibs)

    def owned(h):
        for copy in t_copies[h]:
            copy.wait()
        where = own_rows(h, col)
        total = t_ref[where, :]
        for d in range(1, nc):
            total = total + tland[d - 1, h * sub : (h + 1) * sub, :]
        xr_ref[where, :] = total

    late = order.index((0, 2)) if parts > 2 else -1

    def service(k):
        if parts > 2:
            if k == late:
                owned(2)
                start_all(gathers[2])
            if k == late + 1:
                owned(3)
                start_all(gathers[3])
        for test, lag, act in ((far == 0, 0, relay_source), (far == 1, 2, relay), (far == 2, 4, relay), (far > 2, 6, relay)):
            if 0 <= k - lag < pieces:
                pl.when(test)(functools.partial(act, k - lag))

    for h in range(parts):
        loads[h].wait()
        where = slice(h * part, (h + 1) * part)
        a, b = split(block[where, :])
        t_ref[where, :] = matmul(a, high_op[...]) + matmul(a, low_op[...]) + matmul(b, high_op[...])
        if h == 0:
            pl.semaphore_wait(barrier, ratio - 1 + 2 * (nc - 1))
        if h < 2:
            start_all(t_copies[h])
        if h == parts - 2:
            operator(row * rows, rows, store_row)

    place = 0
    for i in range(size // BLK):
        blocks = lax.dot_general(
            row_op[:, i * BLK : (i + 1) * BLK], t_ref[:, : (i + 1) * BLK], (((0,), (0,)), ((), ())),
            precision=MID, preferred_element_type=jnp.float32,
        )
        for j in range(i + 1):
            acc[place : place + BLK, :] = blocks[:, j * BLK : (j + 1) * BLK]
            place += BLK
    predicted = jnp.dot(x_ref[...], row_op[...], precision=HI, preferred_element_type=jnp.float32)
    predicted = jnp.where(col == 0, predicted, 0.0)
    acc[place:, :] = jnp.zeros((packed - place, BLK), jnp.float32)
    for i in range(size // BLK):
        acc[place + i : place + i + 1, :] = predicted[:, i * BLK : (i + 1) * BLK]
    start, length, slot = 0, packed, 0
    spots = []
    for level, (n, me, peer) in enumerate(levels):
        segment = length // n
        base = take(n - 1)
        copies = []
        for d in range(1, n):
            other = lax.rem(me + d, n)
            src = acc.at[pl.ds(pl.multiple_of(start + other * segment, 8), segment)]
            dst = land.at[pl.ds(slot + (d - 1) * segment, segment)]
            copies.append(remote(src, dst, base + d - 1, peer(d)))
            copies[-1].start()
        if level == 0:
            owned(0)
        if level == 1:
            owned(1)
            start_all(gathers[0])
        if level == 2:
            start_all(gathers[1])
        service(level)
        start = pl.multiple_of(start + me * segment, 8)
        length = segment
        spots.append((start, segment))
        for copy in copies:
            copy.wait()
        mine = acc[pl.ds(start, segment), :]
        for d in range(1, n):
            mine = mine + land[pl.ds(slot + (d - 1) * segment, segment), :]
        acc[pl.ds(start, segment), :] = mine
        slot += (n - 1) * segment
    full[pl.ds(start, length), :] = acc[pl.ds(start, length), :]

    for level in (2, 1, 0):
        n, me, peer = levels[level]
        begin, segment = spots[level]
        base = take(n - 1)
        copies = []
        for d in range(1, n):
            where = full.at[pl.ds(begin, segment)]
            copies.append(remote(where, where, base + d - 1, peer(d)))
            copies[-1].start()
        if level == 1:
            for h in range(2, parts):
                start_all(t_copies[h])
        service(5 - level)
        for copy in copies:
            copy.wait()

    same = lax.broadcasted_iota(jnp.int32, (BLK, BLK), 0) == lax.broadcasted_iota(jnp.int32, (BLK, BLK), 1)
    width = var_ref.shape[1]
    for index, (i, j) in enumerate(pair_blocks(size)):
        square = full[index * BLK : (index + 1) * BLK, :]
        if i == j:
            lane = i * BLK % width
            diagonal = var_ref[i * BLK // width : i * BLK // width + 1, lane : lane + BLK]
            square = 0.5 * (square + square.T) + jnp.where(same, diagonal, 0.0)
        mat[i * BLK : (i + 1) * BLK, j * BLK : (j + 1) * BLK] = square
        if i != j:
            mat[j * BLK : (j + 1) * BLK, i * BLK : (i + 1) * BLK] = square.T
    mat[:, size:] = jnp.zeros((size, size), jnp.float32)
    tail = len(pair_blocks(size)) * BLK
    pred_ref[...] = full[tail : tail + 8, :]

    factor_inverse(mat, work, lambda slot: service(slot + 6))
    for k in range(6 + 4 * (size // BLK), pieces + 6):
        service(k)
    for h in range(parts):
        for copy in gathers[h]:
            copy.wait_send()

    @pl.when(jnp.logical_not(source))
    def _():
        for h in range(parts):
            for copy in gathers[h]:
                copy.wait_recv()

    inverse = mat[:, size:]
    gain = lax.dot_general(
        xr_ref[...], inverse, (((1,), (1,)), ((), ())), precision=MID, preferred_element_type=jnp.float32
    )
    u_ref[...] = jnp.dot(gain, inverse, precision=MID, preferred_element_type=jnp.float32)

    for e in range(pieces):
        _, up, down, sibs = links(e, False)

        @pl.when(goes_up)
        def _():
            up.wait_send()

        @pl.when(goes_down)
        def _():
            down.wait_send()

        for sib in sibs:
            sib.wait()


def exchange(mesh, packed, covariance, state, cells, weights, variance):
    nr, nc = mesh.shape["row"], mesh.shape["col"]
    ratio = nr // nc
    rows, cols = covariance.shape
    size = cells.shape[0] * cells.shape[2]
    parts = part_count(rows, nc)
    landing, length = 0, packed
    for n in (ratio, nc, nc):
        landing += (n - 1) * (length // n)
        length //= n
    pieces = nc * parts
    sems = 2 * (ratio - 1 + 2 * (nc - 1)) + 2 * parts * (nc - 1) + 2 * pieces + pieces * (ratio - 1)
    f32 = jnp.float32
    vmem = pl.BlockSpec(memory_space=pltpu.VMEM)
    return pl.pallas_call(
        functools.partial(kernel, nr, nc, parts),
        out_shape=(
            jax.ShapeDtypeStruct((rows, size), f32),
            jax.ShapeDtypeStruct((ratio, rows, size), f32),
            jax.ShapeDtypeStruct((8, BLK), f32),
        ),
        in_specs=[pl.BlockSpec(memory_space=pl.ANY)] + [vmem] * 4,
        out_specs=(vmem,) * 3,
        scratch_shapes=[
            pltpu.VMEM((rows, cols), f32),
            pltpu.VMEM((cols, size), jnp.bfloat16),
            pltpu.VMEM((cols, size), jnp.bfloat16),
            pltpu.VMEM((rows, size), f32),
            pltpu.VMEM((rows, size), f32),
            pltpu.VMEM((rows, size), f32),
            pltpu.VMEM((packed, BLK), f32),
            pltpu.VMEM((packed, BLK), f32),
            pltpu.VMEM((landing, BLK), f32),
            pltpu.VMEM((nc - 1, rows // nc, size), f32),
            pltpu.VMEM((size, 2 * size), f32),
            pltpu.VMEM((BLK, 2 * BLK), f32),
            pltpu.SemaphoreType.DMA((sems,)),
            pltpu.SemaphoreType.DMA((sems,)),
            pltpu.SemaphoreType.DMA((parts,)),
        ],
        compiler_params=pltpu.CompilerParams(collective_id=0, has_side_effects=True, vmem_limit_bytes=48 * 1024 * 1024),
    )(covariance, state, cells, weights, variance)


def dot(a, b, precision):
    return jnp.dot(a, b, precision=precision, preferred_element_type=jnp.float32)


def on_device(mesh, covariance, state_mean, obs_values, obs_cells, obs_weights, obs_variance):
    rows_dev, cols_dev = covariance.shape
    devices = mesh.shape["row"] * mesh.shape["col"]
    batches, foot, width = obs_cells.shape
    total = batches * width
    filled = len(pair_blocks(total)) * BLK + 8
    unit = 8 * devices
    packed = -(-(filled + 8) // unit) * unit
    u, cross_cols, pred = exchange(mesh, packed, covariance, state_mean.reshape(1, rows_dev), obs_cells, obs_weights, obs_variance)
    innov = obs_values.reshape(total) - pred[: total // BLK].reshape(total)
    mean = state_mean + jnp.sum(u * innov[None, :], axis=1)
    matrix = covariance - dot(u, cross_cols.reshape(cols_dev, total).T, MID)
    return (matrix, mean)


def solution(mesh):
    return jax.shard_map(
        functools.partial(on_device, mesh),
        mesh=mesh,
        in_specs=(P("row", "col"), P("row"), P(), P(), P(), P()),
        out_specs=(P("row", "col"), P("row")),
        check_vma=False,
    )
```

```python
import functools

import jax
import jax.numpy as jnp
from jax import lax
from jax.experimental import pallas as pl
from jax.experimental.pallas import tpu as pltpu
from jax.sharding import PartitionSpec as P

HI = lax.Precision.HIGHEST
MID = lax.Precision.HIGH
MESH = pl.DeviceIdType.MESH
BLK = 128
SUB = 8
PANEL = 32
UNITS = 4

def base_inverse(work, hook):
    tiles = PANEL // SUB

    def panel_step(first, g, carry):
        start = pl.multiple_of(g * PANEL, PANEL)
        panel = work[pl.ds(start, PANEL), :]
        square = pltpu.roll(panel[:, :BLK], BLK - start, 1)[:, :PANEL]
        rows = [slice(t * SUB, (t + 1) * SUB) for t in range(tiles)]
        wide = [[jnp.broadcast_to(square[rows[t], j : j + 1], (SUB, BLK)) for t in range(tiles)] for j in range(PANEL)]
        left = [panel[rows[t], :BLK] for t in range(tiles)]
        right = [panel[rows[t], BLK:] for t in range(tiles)]
        below = lax.broadcasted_iota(jnp.int32, (SUB, BLK), 0)
        scale = [jnp.zeros((SUB, BLK), jnp.float32) for t in range(tiles)]
        for j in range(PANEL):
            home, at = j // SUB, j % SUB
            line = slice(at, at + 1)
            pivot = jnp.broadcast_to(wide[j][home][line, :], (SUB, BLK))
            root = lax.rsqrt(pivot)
            scale[home] = jnp.where(below == at, root, scale[home])
            pivot_left, pivot_right = left[home][line, :], right[home][line, :]
            pivot_wide = [wide[k][home][line, :] for k in range(PANEL)]
            for t in range(home, tiles):
                ratio = wide[j][t] * (1.0 / pivot)
                if t == home:
                    ratio = jnp.where(below > at, ratio, 0.0)
                left[t] = left[t] - ratio * pivot_left
                right[t] = right[t] - ratio * pivot_right
                for k in range(j + 1, PANEL):
                    wide[k][t] = wide[k][t] - ratio * pivot_wide[k]
        left = jnp.concatenate([left[t] * scale[t] for t in range(tiles)], axis=0)
        right = jnp.concatenate([right[t] * scale[t] for t in range(tiles)], axis=0)
        both = jnp.concatenate([left, right], axis=1)
        lane = lax.broadcasted_iota(jnp.int32, (PANEL, BLK), 1)
        lhs = jnp.where(lane >= start + PANEL, left, 0.0)
        work[pl.ds(start, PANEL), :] = both
        work[first:, :] = work[first:, :] - lax.dot_general(lhs[:, first:], both, (((0,), (0,)), ((), ())), precision=HI, preferred_element_type=jnp.float32)
        return carry

    steps = BLK // PANEL // 4
    for quarter in range(4):
        hook(quarter)
        first = quarter * steps * PANEL
        lax.fori_loop(quarter * steps, (quarter + 1) * steps, functools.partial(panel_step, first), 0)


def factor_inverse(mat, work, hook, ready):
    size = mat.shape[0]
    eye = (lax.broadcasted_iota(jnp.int32, (BLK, BLK), 0) == lax.broadcasted_iota(jnp.int32, (BLK, BLK), 1)).astype(jnp.float32)
    for b in range(size // BLK):
        lo, hi = b * BLK, (b + 1) * BLK
        work[:, :BLK] = mat[lo:hi, lo:hi]
        work[:, BLK:] = eye
        base_inverse(work, lambda quarter: hook(4 * b + quarter))
        winv = work[:, BLK:]
        ready(b)
        if hi < size:
            panel = jnp.dot(winv, mat[lo:hi, hi:size], precision=HI, preferred_element_type=jnp.float32)
        if lo > 0:
            left = jnp.dot(winv, mat[lo:hi, size : size + lo], precision=HI, preferred_element_type=jnp.float32)
            mat[lo:hi, size : size + lo] = left
        mat[lo:hi, size + lo : size + hi] = winv
        if hi < size:
            right = mat[lo:hi, size : size + hi]
            dims = (((0,), (0,)), ((), ()))
            mat[hi:size, hi:size] = mat[hi:size, hi:size] - lax.dot_general(panel, panel, dims, precision=HI, preferred_element_type=jnp.float32)
            mat[hi:size, size : size + hi] = mat[hi:size, size : size + hi] - lax.dot_general(panel, right, dims, precision=HI, preferred_element_type=jnp.float32)


def pair_blocks(size):
    count = size // BLK
    return [(i, j) for i in range(count) for j in range(i + 1)]


def split(value):
    high = value.astype(jnp.bfloat16)
    return high, (value - high.astype(jnp.float32)).astype(jnp.bfloat16)


def matmul(a, b, dims=(((1,), (0,)), ((), ()))):
    return lax.dot_general(a, b, dims, preferred_element_type=jnp.float32)


def part_count(rows, nc):
    return 4 if rows % (4 * nc * SUB) == 0 else 2


def plane_shape(nc):
    flat = max(d for d in range(1, nc + 1) if nc % d == 0 and d * d <= nc)
    return nc // flat, flat


def relay_order(nc, parts):
    order = []
    for pair in range(0, parts, 2):
        order += [(0, pair), (0, pair + 1)]
        order += [(d, h) for h in (pair, pair + 1) for d in range(1, nc)]
    return order


def kernel(
    nr, nc, parts, batches, foot, p_ref, pack_ref, u_out, xc_ref, innov_ref,
    u_ref, keep_sem, block, high_op, low_op, row_op, t_ref, xr_ref, acc0, full0, land0, acc1, full1, land1,
    tland, land_a, land_b, mid_a, mid_b, next_a, next_b, mat, work, send_sem, recv_sem, load_sem,
):
    ratio = nr // nc
    row, col = lax.axis_index("row"), lax.axis_index("col")
    high, low = row // ratio, row % ratio
    rows, size = t_ref.shape
    wide = block.shape[1]
    part = rows // parts
    sub = part // nc
    order = relay_order(nc, parts)
    pieces = len(order)
    used = [0]

    def take(count):
        used[0] += count
        return used[0] - count

    width = pack_ref.shape[1]
    listed = batches * foot
    var_row, value_row, state_row = 2 * listed, 2 * listed + batches, 2 * listed + 2 * batches
    loads = []
    for h in range(parts):
        where = pl.ds(h * part, part)
        loads.append(pltpu.make_async_copy(p_ref.at[where], block.at[where], load_sem.at[h]))
        loads[-1].start()

    levels = [
        (ratio, low, lambda d: (high * ratio + lax.rem(low + d, ratio), col)),
        (nc, col, lambda d: (row, lax.rem(col + d, nc))),
        (nc, high, lambda d: (lax.rem(high + d, nc) * ratio + low, col)),
    ]
    barrier = pltpu.get_barrier_semaphore()
    for n, me, peer in levels:
        for d in range(1, n):
            pl.semaphore_signal(barrier, inc=1, device_id=peer(d), device_id_type=MESH)

    def operator(first, count, store):
        step = min(count, BLK)

        def fill(g, carry):
            start = pl.multiple_of(g * step, step)
            place = (lax.broadcasted_iota(jnp.int32, (step, width), 0) + (first + start)).astype(jnp.float32)
            for b in range(batches):
                total = jnp.zeros((step, width), jnp.float32)
                for f in range(foot):
                    at = b * foot + f
                    weight = pack_ref[listed + at : listed + at + 1, :]
                    total = total + jnp.where(pack_ref[at : at + 1, :] == place, weight, 0.0)
                store(start, step, b * width, width, total)
            return carry

        lax.fori_loop(0, count // step, fill, 0)

    def store_col(start, step, lane, width, total):
        h, l = split(total)
        high_op[pl.ds(start, step), lane : lane + width] = h
        low_op[pl.ds(start, step), lane : lane + width] = l

    def store_row(start, step, lane, width, total):
        row_op[pl.ds(start, step), lane : lane + width] = total

    operator(col * wide, wide, store_col)

    def remote(src, dst, sem, device):
        return pltpu.make_async_remote_copy(
            src_ref=src, dst_ref=dst, send_sem=send_sem.at[sem], recv_sem=recv_sem.at[sem],
            device_id=device, device_id_type=MESH,
        )

    def own_rows(h, owner):
        return pl.ds(pl.multiple_of(h * part + owner * sub, 8), sub)

    _, _, col_peer = levels[1]
    _, _, low_peer = levels[0]
    tall, flat = plane_shape(nc)
    hi, lo = col // flat, col % flat
    half = size // 2
    left, right = pl.ds(0, half), pl.ds(half, half)
    chain_base = take(pieces)
    sib_base = take(ratio - 1)
    up_sem, down_sem = sib_base + ratio - 1, sib_base + ratio
    take(2)

    def lo_peer(d):
        return (row, hi * flat + lax.rem(lo + d, flat))

    def hi_peer(d):
        return (row, lax.rem(hi + d, tall) * flat + lo)

    def plane_copies(h):
        stages = scatter, settle, spread, pass_on = [], [], [], []
        base = take(len(stages))

        def add(group, src, dst, device):
            stage = [n for n in range(len(stages)) if stages[n] is group][0]
            group.append(remote(src, dst, base + stage, device))

        own = own_rows(h, col)
        for d in range(1, flat):
            other = lax.rem(lo + d, flat)
            for k in range(tall):
                add(scatter, t_ref.at[own_rows(h, k * flat + other), left], land_a.at[h, d - 1, k], lo_peer(d))
            add(settle, mid_b.at[h, other], next_b.at[h, d - 1], lo_peer(d))
            add(spread, xr_ref.at[own, left], xr_ref.at[own, left], lo_peer(d))
            for k in range(tall):
                where = own_rows(h, k * flat + lo)
                add(pass_on, xr_ref.at[where, right], xr_ref.at[where, right], lo_peer(d))
        for d in range(1, tall):
            other = lax.rem(hi + d, tall)
            for k in range(flat):
                add(scatter, t_ref.at[own_rows(h, other * flat + k), right], land_b.at[h, d - 1, k], hi_peer(d))
            add(settle, mid_a.at[h, other], next_a.at[h, d - 1], hi_peer(d))
            add(spread, xr_ref.at[own, right], xr_ref.at[own, right], hi_peer(d))
            for k in range(flat):
                where = own_rows(h, hi * flat + k)
                add(pass_on, xr_ref.at[where, left], xr_ref.at[where, left], hi_peer(d))
        near = (flat - 1) + (tall - 1)
        wide_count = (flat - 1) * tall + (tall - 1) * flat
        ends = []
        for stage, count in enumerate((wide_count, near, near, wide_count)):
            every = tland.at[pl.ds(0, count * sub // 2)]
            ends.append(remote(every, every, base + stage, lo_peer(1)))
        return stages, ends

    plane = [plane_copies(h) for h in range(parts)]

    def start_all(copies):
        for copy in copies:
            copy.start()

    def scatter(h):
        start_all(plane[h][0][0])

    def settle(h):
        plane[h][1][0].wait()
        for k in range(tall):
            total = t_ref[own_rows(h, k * flat + lo), left]
            for d in range(1, flat):
                total = total + land_a[h, d - 1, k]
            mid_a[h, k] = total
        for k in range(flat):
            total = t_ref[own_rows(h, hi * flat + k), right]
            for d in range(1, tall):
                total = total + land_b[h, d - 1, k]
            mid_b[h, k] = total
        start_all(plane[h][0][1])

    def spread(h):
        plane[h][1][1].wait()
        total = mid_a[h, hi]
        for d in range(1, tall):
            total = total + next_a[h, d - 1]
        xr_ref[own_rows(h, col), left] = total
        total = mid_b[h, lo]
        for d in range(1, flat):
            total = total + next_b[h, d - 1]
        xr_ref[own_rows(h, col), right] = total
        start_all(plane[h][0][2])

    def pass_on(h):
        plane[h][1][2].wait()
        start_all(plane[h][0][3])

    def arrive(h):
        plane[h][1][3].wait_recv()

    source = high == col
    far = jnp.abs(high - col)
    top = nc - 1
    above = (jnp.minimum(high + 1, top) * ratio + low, col)
    below = (jnp.maximum(high - 1, 0) * ratio + low, col)
    goes_up = jnp.logical_and(high >= col, high < top)
    goes_down = jnp.logical_and(high <= col, high > 0)

    def onward(where, src, e):
        dst = xc_ref.at[low, where]
        up = pltpu.make_async_remote_copy(
            src_ref=src, dst_ref=dst, send_sem=send_sem.at[up_sem], recv_sem=recv_sem.at[chain_base + e],
            device_id=above, device_id_type=MESH,
        )
        down = pltpu.make_async_remote_copy(
            src_ref=src, dst_ref=dst, send_sem=send_sem.at[down_sem], recv_sem=recv_sem.at[chain_base + e],
            device_id=below, device_id_type=MESH,
        )
        sibs = [remote(src, dst, sib_base + q - 1, low_peer(q)) for q in range(1, ratio)]
        return up, down, sibs

    def links(e, src_is_own):
        d, h = order[e]
        where = own_rows(h, lax.rem(col - d + nc, nc))
        src = xr_ref.at[where] if src_is_own else xc_ref.at[low, where]
        return (where,) + onward(where, src, e)

    def send_on(up, down, sibs):
        @pl.when(goes_up)
        def _():
            up.start()

        @pl.when(goes_down)
        def _():
            down.start()

        for sib in sibs:
            sib.start()

    def keep(e):
        d, h = order[e]
        where = own_rows(h, lax.rem(col - d + nc, nc))
        return pltpu.make_async_copy(xr_ref.at[where], xc_ref.at[low, where], keep_sem.at[0])

    def relay_source(e):
        d, h = order[e]
        where, up, down, sibs = links(e, True)
        send_on(up, down, sibs)
        keep(e).start()

    def relay(e):
        where, up, down, sibs = links(e, False)
        up.wait_recv()
        send_on(up, down, sibs)

    def emit(pieces_now):
        @pl.when(source)
        def _():
            for e in pieces_now:
                relay_source(e)

    def group(h):
        return [e for e in range(pieces) if order[e][1] == h and order[e][0] > 0]

    def own(h):
        return [order.index((0, h))]

    def point(k):
        for test, lag in ((far == 1, 0), (far == 2, 2), (far > 2, 4)):
            if 0 <= k - lag < pieces:
                pl.when(test)(functools.partial(relay, k - lag))

    for h in range(parts):
        loads[h].wait()
        where = slice(h * part, (h + 1) * part)
        a, b = split(block[where, :])
        t_ref[where, :] = matmul(a, high_op[...]) + matmul(a, low_op[...]) + matmul(b, high_op[...])
        if h == 0:
            pl.semaphore_wait(barrier, ratio - 1 + 2 * (nc - 1))
        if h < 2:
            scatter(h)
        if h == parts - 2:
            operator(row * rows, rows, store_row)

    def reduced(acc, full, land, spread):
        start, length, slot = 0, acc.shape[0], 0
        spots = []

        def exchange_all(level, pairs, count):
            n, me, peer = levels[level]
            base = take(1)
            for d in range(1, n):
                src, dst = pairs(d)
                remote(src, dst, base, peer(d)).start()
            every = land.at[pl.ds(0, (n - 1) * count)]
            return remote(every, every, base, peer(1))

        for level, (n, me, peer) in enumerate(levels):
            whole = level == 2 and not spread
            segment = length if whole else length // n

            def scattered(d):
                begin = start if whole else pl.multiple_of(start + lax.rem(me + d, n) * segment, 8)
                return acc.at[pl.ds(begin, segment)], land.at[pl.ds(slot + (d - 1) * segment, segment)]

            end = exchange_all(level, scattered, segment)
            yield
            if not whole:
                start = pl.multiple_of(start + me * segment, 8)
                spots.append((start, segment))
            length = segment
            end.wait()
            where = pl.ds(start, length)
            mine = acc[where, :]
            for d in range(1, n):
                mine = mine + land[pl.ds(slot + (d - 1) * segment, segment), :]
            slot += (n - 1) * segment
            if level == 2:
                full[where, :] = mine
            else:
                acc[where, :] = mine
        for level in (2, 1, 0) if spread else (1, 0):
            begin, segment = spots[level]
            where = full.at[pl.ds(begin, segment)]
            end = exchange_all(level, lambda d: (where, where), segment)
            yield
            end.wait()
        yield

    def sums(i):
        return lax.dot_general(
            row_op[:, i * BLK : (i + 1) * BLK], t_ref[:, : (i + 1) * BLK], (((0,), (0,)), ((), ())),
            precision=MID, preferred_element_type=jnp.float32,
        )

    first = reduced(acc0, full0, land0, False)
    rest = reduced(acc1, full1, land1, True)
    place = 0
    settle(0)
    for i in range(size // BLK):
        blocks = sums(i)
        if i == 0:
            acc0[:BLK, :] = blocks
            if acc0.shape[0] > BLK:
                acc0[BLK:, :] = jnp.zeros((acc0.shape[0] - BLK, BLK), jnp.float32)
            next(first)
            continue
        for j in range(i + 1):
            acc1[place : place + BLK, :] = blocks[:, j * BLK : (j + 1) * BLK]
            place += BLK
        if i == 1:
            next(first)
            settle(1)
        if i == 2:
            spread(0)
            next(first)
            emit(own(0))
    predicted = jnp.zeros((1, size), jnp.float32)
    for q in range(rows // width):
        state = pack_ref[state_row + q : state_row + q + 1, :]
        predicted = predicted + jnp.dot(
            state, row_op[q * width : (q + 1) * width, :], precision=HI, preferred_element_type=jnp.float32
        )
    predicted = jnp.where(col == 0, predicted, 0.0)
    acc1[place:, :] = jnp.zeros((acc1.shape[0] - place, BLK), jnp.float32)
    for i in range(size // BLK):
        acc1[place + i : place + i + 1, :] = predicted[:, i * BLK : (i + 1) * BLK]
    next(rest)
    spread(1)
    pass_on(0)
    emit(own(1))
    next(first)
    next(rest)
    pass_on(1)
    arrive(0)
    emit(group(0)[:1])
    next(first)
    point(0)
    next(first)
    next(rest)
    emit(group(0)[1:])
    if parts > 2:
        scatter(2)
    point(1)

    same = lax.broadcasted_iota(jnp.int32, (BLK, BLK), 0) == lax.broadcasted_iota(jnp.int32, (BLK, BLK), 1)

    def place_block(i, j, square):
        if i == j:
            lane = i * BLK % width
            line = var_row + i * BLK // width
            diagonal = pack_ref[line : line + 1, lane : lane + BLK]
            square = 0.5 * (square + square.T) + jnp.where(same, diagonal, 0.0)
        mat[i * BLK : (i + 1) * BLK, j * BLK : (j + 1) * BLK] = square
        if i != j:
            mat[j * BLK : (j + 1) * BLK, i * BLK : (i + 1) * BLK] = square.T

    place_block(0, 0, full0[:BLK, :])
    mat[:, size:] = jnp.zeros((size, size), jnp.float32)

    points = {2: 2, 4: 6, 6: 7, 7: 8, 8: 9, 10: 10, 12: 11, 14: 12}

    def hook(slot):
        if slot == 1:
            next(rest)
        if slot == 3:
            arrive(1)
            emit(group(1))
        if parts > 2:
            if slot == 2:
                scatter(3)
            if slot == 3:
                settle(2)
            if slot == 5:
                spread(3)
                emit(own(3))
                pass_on(2)
            if slot == 7:
                pass_on(3)
                arrive(2)
                emit(group(2))
            if slot == 10:
                arrive(3)
                emit(group(3))
        if slot in points:
            point(points[slot])

    def ready(b):
        if b == 0:
            next(rest)
            point(3)
            next(rest)
            if parts > 2:
                spread(2)
                emit(own(2))
                settle(3)
            point(4)
            next(rest)
            point(5)
            for index, (i, j) in enumerate(pair_blocks(size)[1:]):
                place_block(i, j, full1[index * BLK : (index + 1) * BLK, :])
            innov_ref[...] = jnp.zeros((8, BLK), jnp.float32)
            for i in range(size // BLK):
                lane = i * BLK % width
                line = value_row + i * BLK // width
                value = pack_ref[line : line + 1, lane : lane + BLK]
                innov_ref[i : i + 1, :] = value - full1[place + i : place + i + 1, :]

    factor_inverse(mat, work, hook, ready)
    done = [13]

    def advance(last):
        while done[0] <= last:
            point(done[0])
            done[0] += 1

    advance(13)
    middle = size // 2
    across, along = (((1,), (1,)), ((), ())), (((1,), (0,)), ((), ()))
    high_w, low_w = split(mat[:, size:])

    def product(value, rows_w, lanes_w, dims):
        a, b = split(value)
        c, d = high_w[rows_w, lanes_w], low_w[rows_w, lanes_w]
        return matmul(a, c, dims) + matmul(a, d, dims) + matmul(b, c, dims)

    lower, upper, every = slice(0, middle), slice(middle, size), slice(0, size)
    step = rows // UNITS
    results = []
    for c in range(UNITS):
        where = slice(c * step, (c + 1) * step)
        gain_left = product(xr_ref[where, lower], lower, lower, across)
        gain_right = product(xr_ref[where, :], upper, every, across)
        u_ref[where, lower] = product(jnp.concatenate([gain_left, gain_right], axis=1), every, lower, along)
        u_ref[where, upper] = product(gain_right, upper, upper, along)
        results.append(pltpu.make_async_copy(u_ref.at[pl.ds(c * step, step)], u_out.at[pl.ds(c * step, step)], keep_sem.at[1]))
        results[-1].start()
        if c % 2 == 1:
            advance(done[0])
    advance(pieces + 3)
    pltpu.make_async_copy(u_ref, u_out, keep_sem.at[1]).wait()
    everything = pl.ds(0, rows)

    @pl.when(source)
    def _():
        pltpu.make_async_copy(xr_ref, xc_ref.at[low], keep_sem.at[0]).wait()

    for h in range(parts):
        plane[h][1][3].wait_send()
    up, down, sibs = onward(everything, xr_ref, 0)

    @pl.when(goes_up)
    def _():
        up.wait_send()

    @pl.when(goes_down)
    def _():
        down.wait_send()

    for sib in sibs:
        sib.wait()


def padded(count, unit):
    return -(-count // unit) * unit


def exchange(mesh, covariance, pack, batches, foot):
    nr, nc = mesh.shape["row"], mesh.shape["col"]
    ratio = nr // nc
    rows, cols = covariance.shape
    size = batches * pack.shape[1]
    parts = part_count(rows, nc)
    group = ratio * nc
    lead = padded(BLK, 8 * group)
    follow = padded((len(pair_blocks(size)) - 1) * BLK + 8, 8 * group * nc)
    half, quarter = follow // ratio, follow // group
    land0 = (ratio - 1) * (lead // ratio) + 2 * (nc - 1) * (lead // group)
    land1 = (ratio - 1) * half + (nc - 1) * quarter + (nc - 1) * (quarter // nc)
    tall, flat = plane_shape(nc)
    sub = rows // (parts * nc)
    pieces = nc * parts
    sems = 2 * 2 * 3 + 4 * parts + pieces + ratio + 1
    f32 = jnp.float32
    vmem = pl.BlockSpec(memory_space=pltpu.VMEM)
    return pl.pallas_call(
        functools.partial(kernel, nr, nc, parts, batches, foot),
        out_shape=(
            jax.ShapeDtypeStruct((rows, size), f32),
            jax.ShapeDtypeStruct((ratio, rows, size), f32),
            jax.ShapeDtypeStruct((8, BLK), f32),
        ),
        in_specs=[pl.BlockSpec(memory_space=pl.ANY), vmem],
        out_specs=(pl.BlockSpec(memory_space=pl.ANY),) * 2 + (vmem,),
        scratch_shapes=[
            pltpu.VMEM((rows, size), f32),
            pltpu.SemaphoreType.DMA((2,)),
            pltpu.VMEM((rows, cols), f32),
            pltpu.VMEM((cols, size), jnp.bfloat16),
            pltpu.VMEM((cols, size), jnp.bfloat16),
            pltpu.VMEM((rows, size), f32),
            pltpu.VMEM((rows, size), f32),
            pltpu.VMEM((rows, size), f32),
            pltpu.VMEM((lead, BLK), f32),
            pltpu.VMEM((lead, BLK), f32),
            pltpu.VMEM((land0, BLK), f32),
            pltpu.VMEM((follow, BLK), f32),
            pltpu.VMEM((follow, BLK), f32),
            pltpu.VMEM((land1, BLK), f32),
            pltpu.VMEM(((flat - 1) * tall * sub, size), f32),
            pltpu.VMEM((parts, flat - 1, tall, sub, size // 2), f32),
            pltpu.VMEM((parts, tall - 1, flat, sub, size // 2), f32),
            pltpu.VMEM((parts, tall, sub, size // 2), f32),
            pltpu.VMEM((parts, flat, sub, size // 2), f32),
            pltpu.VMEM((parts, tall - 1, sub, size // 2), f32),
            pltpu.VMEM((parts, flat - 1, sub, size // 2), f32),
            pltpu.VMEM((size, 2 * size), f32),
            pltpu.VMEM((BLK, 2 * BLK), f32),
            pltpu.SemaphoreType.DMA((sems,)),
            pltpu.SemaphoreType.DMA((sems,)),
            pltpu.SemaphoreType.DMA((parts,)),
        ],
        compiler_params=pltpu.CompilerParams(collective_id=0, has_side_effects=True, vmem_limit_bytes=40 * 1024 * 1024),
    )(covariance, pack)


def on_device(mesh, covariance, state_mean, obs_values, obs_cells, obs_weights, obs_variance):
    rows_dev, cols_dev = covariance.shape
    batches, foot, width = obs_cells.shape
    total = batches * width
    pack = jnp.concatenate(
        [
            obs_cells.astype(jnp.float32).reshape(batches * foot, width),
            obs_weights.reshape(batches * foot, width),
            obs_variance,
            obs_values,
            state_mean.reshape(rows_dev // width, width),
        ],
        axis=0,
    )
    u, cross_cols, innov = exchange(mesh, covariance, pack, batches, foot)
    innov = innov[: total // BLK].reshape(total)
    mean = state_mean + jnp.sum(u * innov[None, :], axis=1)
    update = jnp.dot(u, cross_cols.reshape(cols_dev, total).T, precision=MID, preferred_element_type=jnp.float32)
    return (covariance - update, mean)


def solution(mesh):
    return jax.shard_map(
        functools.partial(on_device, mesh),
        mesh=mesh,
        in_specs=(P("row", "col"), P("row"), P(), P(), P(), P()),
        out_specs=(P("row", "col"), P("row")),
        check_vma=False,
    )
```

```python
import functools

import jax
import jax.numpy as jnp
from jax import lax
from jax.experimental import pallas as pl
from jax.experimental.pallas import tpu as pltpu
from jax.sharding import PartitionSpec as P

HI = lax.Precision.HIGHEST
MID = lax.Precision.HIGH
MESH = pl.DeviceIdType.MESH
BLK = 128
SUB = 8
PANEL = 32
UNITS = 2

def base_inverse(work, hook):
    tiles = PANEL // SUB

    def panel_step(first, g, carry):
        start = pl.multiple_of(g * PANEL, PANEL)
        panel = work[pl.ds(start, PANEL), :]
        square = pltpu.roll(panel[:, :BLK], BLK - start, 1)[:, :PANEL]
        rows = [slice(t * SUB, (t + 1) * SUB) for t in range(tiles)]
        wide = [[jnp.broadcast_to(square[rows[t], j : j + 1], (SUB, BLK)) for t in range(tiles)] for j in range(PANEL)]
        left = [panel[rows[t], :BLK] for t in range(tiles)]
        right = [panel[rows[t], BLK:] for t in range(tiles)]
        below = lax.broadcasted_iota(jnp.int32, (SUB, BLK), 0)
        scale = [jnp.zeros((SUB, BLK), jnp.float32) for t in range(tiles)]
        for j in range(PANEL):
            home, at = j // SUB, j % SUB
            line = slice(at, at + 1)
            pivot = jnp.broadcast_to(wide[j][home][line, :], (SUB, BLK))
            root = lax.rsqrt(pivot)
            scale[home] = jnp.where(below == at, root, scale[home])
            pivot_left, pivot_right = left[home][line, :], right[home][line, :]
            pivot_wide = [wide[k][home][line, :] for k in range(PANEL)]
            for t in range(home, tiles):
                ratio = wide[j][t] * (1.0 / pivot)
                if t == home:
                    ratio = jnp.where(below > at, ratio, 0.0)
                left[t] = left[t] - ratio * pivot_left
                right[t] = right[t] - ratio * pivot_right
                for k in range(j + 1, PANEL):
                    wide[k][t] = wide[k][t] - ratio * pivot_wide[k]
        left = jnp.concatenate([left[t] * scale[t] for t in range(tiles)], axis=0)
        right = jnp.concatenate([right[t] * scale[t] for t in range(tiles)], axis=0)
        both = jnp.concatenate([left, right], axis=1)
        lane = lax.broadcasted_iota(jnp.int32, (PANEL, BLK), 1)
        lhs = jnp.where(lane >= start + PANEL, left, 0.0)
        work[pl.ds(start, PANEL), :] = both
        work[first:, :] = work[first:, :] - lax.dot_general(lhs[:, first:], both, (((0,), (0,)), ((), ())), precision=HI, preferred_element_type=jnp.float32)
        return carry

    steps = BLK // PANEL // 4
    for quarter in range(4):
        hook(quarter)
        first = quarter * steps * PANEL
        lax.fori_loop(quarter * steps, (quarter + 1) * steps, functools.partial(panel_step, first), 0)


def factor_inverse(mat, work, hook, ready):
    size = mat.shape[0]
    eye = (lax.broadcasted_iota(jnp.int32, (BLK, BLK), 0) == lax.broadcasted_iota(jnp.int32, (BLK, BLK), 1)).astype(jnp.float32)
    for b in range(size // BLK):
        lo, hi = b * BLK, (b + 1) * BLK
        work[:, :BLK] = mat[lo:hi, lo:hi]
        work[:, BLK:] = eye
        base_inverse(work, lambda quarter: hook(4 * b + quarter))
        winv = work[:, BLK:]
        ready(b)
        if hi < size:
            panel = jnp.dot(winv, mat[lo:hi, hi:size], precision=HI, preferred_element_type=jnp.float32)
        if lo > 0:
            left = jnp.dot(winv, mat[lo:hi, size : size + lo], precision=HI, preferred_element_type=jnp.float32)
            mat[lo:hi, size : size + lo] = left
        mat[lo:hi, size + lo : size + hi] = winv
        if hi < size:
            right = mat[lo:hi, size : size + hi]
            dims = (((0,), (0,)), ((), ()))
            mat[hi:size, hi:size] = mat[hi:size, hi:size] - lax.dot_general(panel, panel, dims, precision=HI, preferred_element_type=jnp.float32)
            mat[hi:size, size : size + hi] = mat[hi:size, size : size + hi] - lax.dot_general(panel, right, dims, precision=HI, preferred_element_type=jnp.float32)


def pair_blocks(size):
    count = size // BLK
    return [(i, j) for i in range(count) for j in range(i + 1)]


def split(value):
    high = value.astype(jnp.bfloat16)
    return high, (value - high.astype(jnp.float32)).astype(jnp.bfloat16)


def matmul(a, b, dims=(((1,), (0,)), ((), ()))):
    return lax.dot_general(a, b, dims, preferred_element_type=jnp.float32)


def part_count(rows, nc):
    return 4 if rows % (4 * nc * SUB) == 0 else 2


def plane_shape(nc):
    flat = max(d for d in range(1, nc + 1) if nc % d == 0 and d * d <= nc)
    return nc // flat, flat


def relay_order(nc, parts):
    order = []
    for pair in range(0, parts, 2):
        order += [(0, pair), (0, pair + 1)]
        order += [(d, h) for h in (pair, pair + 1) for d in range(1, nc)]
    return order


def kernel(
    nr, nc, parts, batches, foot, p_ref, pack_ref, u_out, xc_ref, innov_ref,
    u_ref, keep_sem, block, high_op, low_op, row_op, t_ref, xr_ref, acc0, full0, land0, acc1, full1, land1,
    side_ref, tland, land_a, land_b, mid_a, mid_b, next_a, next_b, mat, work, send_sem, recv_sem, load_sem,
):
    ratio = nr // nc
    row, col = lax.axis_index("row"), lax.axis_index("col")
    high, low = row // ratio, row % ratio
    rows, size = t_ref.shape
    wide = block.shape[1]
    part = rows // parts
    sub = part // nc
    order = relay_order(nc, parts)
    pieces = len(order)
    used = [0]

    def take(count):
        used[0] += count
        return used[0] - count

    width = pack_ref.shape[1]
    listed = batches * foot
    var_row, value_row, state_row = 2 * listed, 2 * listed + batches, 2 * listed + 2 * batches
    loads = []
    for h in range(parts):
        where = pl.ds(h * part, part)
        loads.append(pltpu.make_async_copy(p_ref.at[where], block.at[where], load_sem.at[h]))
        loads[-1].start()

    levels = [
        (ratio, low, lambda d: (high * ratio + lax.rem(low + d, ratio), col)),
        (nc, col, lambda d: (row, lax.rem(col + d, nc))),
        (nc, high, lambda d: (lax.rem(high + d, nc) * ratio + low, col)),
    ]
    barrier = pltpu.get_barrier_semaphore()
    for n, me, peer in levels:
        for d in range(1, n):
            pl.semaphore_signal(barrier, inc=1, device_id=peer(d), device_id_type=MESH)

    def operator(first, count, store):
        step = min(count, BLK)

        def fill(g, carry):
            start = pl.multiple_of(g * step, step)
            place = (lax.broadcasted_iota(jnp.int32, (step, width), 0) + (first + start)).astype(jnp.float32)
            for b in range(batches):
                total = jnp.zeros((step, width), jnp.float32)
                for f in range(foot):
                    at = b * foot + f
                    weight = pack_ref[listed + at : listed + at + 1, :]
                    total = total + jnp.where(pack_ref[at : at + 1, :] == place, weight, 0.0)
                store(start, step, b * width, width, total)
            return carry

        lax.fori_loop(0, count // step, fill, 0)

    def store_col(start, step, lane, width, total):
        h, l = split(total)
        high_op[pl.ds(start, step), lane : lane + width] = h
        low_op[pl.ds(start, step), lane : lane + width] = l

    def store_row(start, step, lane, width, total):
        row_op[pl.ds(start, step), lane : lane + width] = total

    operator(col * wide, wide, store_col)

    def remote(src, dst, sem, device):
        return pltpu.make_async_remote_copy(
            src_ref=src, dst_ref=dst, send_sem=send_sem.at[sem], recv_sem=recv_sem.at[sem],
            device_id=device, device_id_type=MESH,
        )

    def own_rows(h, owner):
        return pl.ds(pl.multiple_of(h * part + owner * sub, 8), sub)

    _, _, col_peer = levels[1]
    _, _, low_peer = levels[0]
    tall, flat = plane_shape(nc)
    hi, lo = col // flat, col % flat
    half = size // 2
    left, right = pl.ds(0, half), pl.ds(half, half)
    chain_base = take(pieces)
    sib_base = take(ratio - 1)
    up_sem, down_sem = sib_base + ratio - 1, sib_base + ratio
    take(2)

    def lo_peer(d):
        return (row, hi * flat + lax.rem(lo + d, flat))

    def hi_peer(d):
        return (row, lax.rem(hi + d, tall) * flat + lo)

    def plane_copies(h):
        stages = scatter, settle, spread, pass_on = [], [], [], []
        base = take(len(stages))

        def add(group, src, dst, device):
            stage = [n for n in range(len(stages)) if stages[n] is group][0]
            group.append(remote(src, dst, base + stage, device))

        own = own_rows(h, col)
        for d in range(1, flat):
            other = lax.rem(lo + d, flat)
            for k in range(tall):
                add(scatter, t_ref.at[own_rows(h, k * flat + other), left], land_a.at[h, d - 1, k], lo_peer(d))
            add(settle, mid_b.at[h, other], next_b.at[h, d - 1], lo_peer(d))
            add(spread, xr_ref.at[own, left], xr_ref.at[own, left], lo_peer(d))
            for k in range(tall):
                where = own_rows(h, k * flat + lo)
                add(pass_on, xr_ref.at[where, right], xr_ref.at[where, right], lo_peer(d))
        for d in range(1, tall):
            other = lax.rem(hi + d, tall)
            for k in range(flat):
                add(scatter, t_ref.at[own_rows(h, other * flat + k), right], land_b.at[h, d - 1, k], hi_peer(d))
            add(settle, mid_a.at[h, other], next_a.at[h, d - 1], hi_peer(d))
            add(spread, xr_ref.at[own, right], xr_ref.at[own, right], hi_peer(d))
            for k in range(flat):
                where = own_rows(h, hi * flat + k)
                add(pass_on, xr_ref.at[where, left], xr_ref.at[where, left], hi_peer(d))
        near = (flat - 1) + (tall - 1)
        wide_count = (flat - 1) * tall + (tall - 1) * flat
        ends = []
        for stage, count in enumerate((wide_count, near, near, wide_count)):
            every = tland.at[pl.ds(0, count * sub // 2)]
            ends.append(remote(every, every, base + stage, lo_peer(1)))
        return stages, ends

    plane = [plane_copies(h) for h in range(parts)]

    def start_all(copies):
        for copy in copies:
            copy.start()

    def scatter(h):
        start_all(plane[h][0][0])

    def settle(h):
        plane[h][1][0].wait()
        for k in range(tall):
            total = t_ref[own_rows(h, k * flat + lo), left]
            for d in range(1, flat):
                total = total + land_a[h, d - 1, k]
            mid_a[h, k] = total
        for k in range(flat):
            total = t_ref[own_rows(h, hi * flat + k), right]
            for d in range(1, tall):
                total = total + land_b[h, d - 1, k]
            mid_b[h, k] = total
        start_all(plane[h][0][1])

    def spread(h):
        plane[h][1][1].wait()
        total = mid_a[h, hi]
        for d in range(1, tall):
            total = total + next_a[h, d - 1]
        xr_ref[own_rows(h, col), left] = total
        total = mid_b[h, lo]
        for d in range(1, flat):
            total = total + next_b[h, d - 1]
        xr_ref[own_rows(h, col), right] = total
        start_all(plane[h][0][2])

    def pass_on(h):
        plane[h][1][2].wait()
        start_all(plane[h][0][3])

    def arrive(h):
        plane[h][1][3].wait_recv()

    source = high == col
    far = jnp.abs(high - col)
    top = nc - 1
    above = (jnp.minimum(high + 1, top) * ratio + low, col)
    below = (jnp.maximum(high - 1, 0) * ratio + low, col)
    goes_up = jnp.logical_and(high >= col, high < top)
    goes_down = jnp.logical_and(high <= col, high > 0)

    def onward(where, src, e):
        dst = xc_ref.at[low, where]
        up = pltpu.make_async_remote_copy(
            src_ref=src, dst_ref=dst, send_sem=send_sem.at[up_sem], recv_sem=recv_sem.at[chain_base + e],
            device_id=above, device_id_type=MESH,
        )
        down = pltpu.make_async_remote_copy(
            src_ref=src, dst_ref=dst, send_sem=send_sem.at[down_sem], recv_sem=recv_sem.at[chain_base + e],
            device_id=below, device_id_type=MESH,
        )
        sibs = [remote(src, dst, sib_base + q - 1, low_peer(q)) for q in range(1, ratio)]
        return up, down, sibs

    def links(e, src_is_own):
        d, h = order[e]
        where = own_rows(h, lax.rem(col - d + nc, nc))
        src = xr_ref.at[where] if src_is_own else xc_ref.at[low, where]
        return (where,) + onward(where, src, e)

    def send_on(e, up, down, sibs):
        owner = lax.rem(col - order[e][0] + nc, nc)

        @pl.when(jnp.logical_and(goes_up, owner != top))
        def _():
            up.start()

        @pl.when(jnp.logical_and(goes_down, owner != 0))
        def _():
            down.start()

        for sib in sibs:
            sib.start()

    def keep(e):
        d, h = order[e]
        where = own_rows(h, lax.rem(col - d + nc, nc))
        return pltpu.make_async_copy(xr_ref.at[where], xc_ref.at[low, where], keep_sem.at[0])

    def relay_source(e):
        d, h = order[e]
        where, up, down, sibs = links(e, True)
        send_on(e, up, down, sibs)
        keep(e).start()

    def relay(e):
        where, up, down, sibs = links(e, False)
        up.wait_recv()
        send_on(e, up, down, sibs)

    side_recv = take(nc * parts)
    side_send = take(2 * nc)
    last_up = jnp.logical_and(col == top, high < top)
    last_down = jnp.logical_and(col == 0, high > 0)

    def side(src, slot, h, lag, device):
        dst = side_ref.at[slot, pl.ds(h * sub, sub)]
        return pltpu.make_async_remote_copy(
            src_ref=src, dst_ref=dst, send_sem=send_sem.at[side_send + lag],
            recv_sem=recv_sem.at[side_recv + slot * parts + h], device_id=device, device_id_type=MESH,
        )

    def deliver(slot, h, lag, upward):
        first = (h // 2) * 2 * nc + 2 + (h % 2) * (nc - 1)
        e = first + (slot if upward else slot - 1)
        return pltpu.make_async_remote_copy(
            src_ref=side_ref.at[slot, pl.ds(h * sub, sub)], dst_ref=xc_ref.at[low, own_rows(h, top if upward else 0)],
            send_sem=send_sem.at[side_send + nc + lag], recv_sem=recv_sem.at[chain_base + e],
            device_id=(row, slot), device_id_type=MESH,
        )

    def side_start(h):
        for test, device in ((last_up, above), (last_down, below)):
            @pl.when(test)
            def _():
                side(xr_ref.at[own_rows(h, col)], high, h, 0, device).start()

    def side_edges(lag):
        up, down = high - lag, high + lag
        return (
            (True, up, jnp.logical_and(col == top, up >= 0), above, high < top),
            (False, down, jnp.logical_and(col == 0, down <= top), below, high > 0),
        )

    def side_forward(h, lag):
        for _, slot, edge, device, onward_too in side_edges(lag):
            @pl.when(edge)
            def _():
                copy = side(side_ref.at[slot, pl.ds(h * sub, sub)], slot, h, lag, device)
                copy.wait_recv()
                pl.when(onward_too)(copy.start)

    def side_deliver(h, lag):
        for upward, slot, edge, _, _ in side_edges(lag):
            pl.when(edge)(deliver(slot, h, lag, upward).start)

    def each_lag(act, h, lag):
        for each in range(lag, nc if lag == 3 else min(lag + 1, nc)):
            act(h, each)

    def side_take(h):
        @pl.when(jnp.logical_not(source))
        def _():
            e = (h // 2) * 2 * nc + 2 + (h % 2) * (nc - 1) + jnp.where(high > col, col, col - 1)
            where = own_rows(h, jnp.where(high > col, top, 0))
            up, _, sibs = onward(where, xc_ref.at[low, where], e)
            up.wait_recv()
            for sib in sibs:
                sib.start()

    def side_drain():
        span = pl.ds(0, parts * sub)
        for upward in (True, False):
            for lag in range(nc):
                slot = high - lag if upward else high + lag
                edge = jnp.logical_and(col == top, slot >= 0) if upward else jnp.logical_and(col == 0, slot <= top)
                whole = pltpu.make_async_remote_copy(
                    src_ref=tland.at[span], dst_ref=tland.at[span], send_sem=send_sem.at[side_send + lag],
                    recv_sem=recv_sem.at[side_recv], device_id=above, device_id_type=MESH,
                )
                pl.when(jnp.logical_and(edge, high < top if upward else high > 0))(whole.wait_send)
                if lag > 0:
                    whole = pltpu.make_async_remote_copy(
                        src_ref=tland.at[span], dst_ref=tland.at[span], send_sem=send_sem.at[side_send + nc + lag],
                        recv_sem=recv_sem.at[side_recv], device_id=above, device_id_type=MESH,
                    )
                    pl.when(edge)(whole.wait_send)

    def emit(pieces_now):
        @pl.when(source)
        def _():
            for e in pieces_now:
                relay_source(e)

    def group(h):
        return [e for e in range(pieces) if order[e][1] == h and order[e][0] > 0]

    def own(h):
        return [order.index((0, h))]

    def point(k):
        for test, lag in ((far == 1, 0), (far == 2, 2), (far > 2, 4)):
            if 0 <= k - lag < pieces:
                owner = lax.rem(col - order[k - lag][0] + nc, nc)
                chained = owner != jnp.where(high > col, top, 0)
                pl.when(jnp.logical_and(test, chained))(functools.partial(relay, k - lag))

    for h in range(parts):
        loads[h].wait()
        where = slice(h * part, (h + 1) * part)
        a, b = split(block[where, :])
        t_ref[where, :] = matmul(a, high_op[...]) + matmul(a, low_op[...]) + matmul(b, high_op[...])
        if h == 0:
            pl.semaphore_wait(barrier, ratio - 1 + 2 * (nc - 1))
        if h < 2:
            scatter(h)
        if h == parts - 2:
            operator(row * rows, rows, store_row)

    def reduced(acc, full, land, spread):
        start, length, slot = 0, acc.shape[0], 0
        spots = []

        def exchange_all(level, pairs, count):
            n, me, peer = levels[level]
            base = take(1)
            for d in range(1, n):
                src, dst = pairs(d)
                remote(src, dst, base, peer(d)).start()
            every = land.at[pl.ds(0, (n - 1) * count)]
            return remote(every, every, base, peer(1))

        for level, (n, me, peer) in enumerate(levels):
            whole = level == 2 and not spread
            segment = length if whole else length // n

            def scattered(d):
                begin = start if whole else pl.multiple_of(start + lax.rem(me + d, n) * segment, 8)
                return acc.at[pl.ds(begin, segment)], land.at[pl.ds(slot + (d - 1) * segment, segment)]

            end = exchange_all(level, scattered, segment)
            yield
            if not whole:
                start = pl.multiple_of(start + me * segment, 8)
                spots.append((start, segment))
            length = segment
            end.wait()
            where = pl.ds(start, length)
            mine = acc[where, :]
            for d in range(1, n):
                mine = mine + land[pl.ds(slot + (d - 1) * segment, segment), :]
            slot += (n - 1) * segment
            if level == 2:
                full[where, :] = mine
            else:
                acc[where, :] = mine
        for level in (2, 1, 0) if spread else (1, 0):
            begin, segment = spots[level]
            where = full.at[pl.ds(begin, segment)]
            end = exchange_all(level, lambda d: (where, where), segment)
            yield
            end.wait()
        yield

    def sums(i):
        return lax.dot_general(
            row_op[:, i * BLK : (i + 1) * BLK], t_ref[:, : (i + 1) * BLK], (((0,), (0,)), ((), ())),
            precision=MID, preferred_element_type=jnp.float32,
        )

    first = reduced(acc0, full0, land0, False)
    rest = reduced(acc1, full1, land1, True)
    place = 0
    settle(0)
    for i in range(size // BLK):
        blocks = sums(i)
        if i == 0:
            acc0[:BLK, :] = blocks
            if acc0.shape[0] > BLK:
                acc0[BLK:, :] = jnp.zeros((acc0.shape[0] - BLK, BLK), jnp.float32)
            next(first)
            continue
        for j in range(i + 1):
            acc1[place : place + BLK, :] = blocks[:, j * BLK : (j + 1) * BLK]
            place += BLK
        if i == 1:
            next(first)
            settle(1)
        if i == 2:
            spread(0)
            next(first)
            emit(own(0))
            side_start(0)
    predicted = jnp.zeros((1, size), jnp.float32)
    for q in range(rows // width):
        state = pack_ref[state_row + q : state_row + q + 1, :]
        predicted = predicted + jnp.dot(
            state, row_op[q * width : (q + 1) * width, :], precision=HI, preferred_element_type=jnp.float32
        )
    predicted = jnp.where(col == 0, predicted, 0.0)
    acc1[place:, :] = jnp.zeros((acc1.shape[0] - place, BLK), jnp.float32)
    for i in range(size // BLK):
        acc1[place + i : place + i + 1, :] = predicted[:, i * BLK : (i + 1) * BLK]
    next(rest)
    spread(1)
    side_start(1)
    pass_on(0)
    emit(own(1))
    next(first)
    next(rest)
    pass_on(1)
    next(first)
    point(0)
    next(first)
    next(rest)
    arrive(0)
    emit(group(0)[:1])
    if parts > 2:
        scatter(2)
        scatter(3)
    point(1)

    same = lax.broadcasted_iota(jnp.int32, (BLK, BLK), 0) == lax.broadcasted_iota(jnp.int32, (BLK, BLK), 1)

    def place_block(i, j, square):
        if i == j:
            lane = i * BLK % width
            line = var_row + i * BLK // width
            diagonal = pack_ref[line : line + 1, lane : lane + BLK]
            square = 0.5 * (square + square.T) + jnp.where(same, diagonal, 0.0)
        mat[i * BLK : (i + 1) * BLK, j * BLK : (j + 1) * BLK] = square
        if i != j:
            mat[j * BLK : (j + 1) * BLK, i * BLK : (i + 1) * BLK] = square.T

    place_block(0, 0, full0[:BLK, :])
    mat[:, size:] = jnp.zeros((size, size), jnp.float32)

    points = {2: 2, 4: 6, 5: 7, 6: 8, 7: 9, 8: 10, 10: 11, 11: 12, 12: 13, 13: 14, 15: 15}

    sides = {
        4: [(side_forward, 0, 2), (side_forward, 1, 2)],
        6: [(side_forward, 2, 1), (side_deliver, 0, 1), (side_deliver, 1, 1)],
        7: [(side_forward, 3, 1)],
        8: [(side_deliver, 0, 2), (side_deliver, 1, 2), (side_forward, 0, 3), (side_forward, 1, 3), (side_deliver, 0, 3), (side_deliver, 1, 3)],
        9: [(side_forward, 2, 2), (side_deliver, 2, 1), (side_deliver, 3, 1)],
        11: [(side_forward, 3, 2)],
        12: [(side_deliver, 2, 2), (side_deliver, 3, 2)],
        14: [(side_forward, 2, 3), (side_deliver, 2, 3)],
        15: [(side_forward, 3, 3), (side_deliver, 3, 3)],
    }

    def hook(slot):
        if slot == 1:
            next(rest)
            emit(group(0)[1:])
            for h in range(2):
                each_lag(side_forward, h, 1)
        if parts > 2 and slot == 2:
            settle(2)
        if slot == 3:
            arrive(1)
            emit(group(1))
        if parts > 2:
            if slot == 3:
                settle(3)
            if slot == 4:
                pass_on(2)
            if slot == 5:
                pass_on(3)
            if slot == 7:
                arrive(2)
                emit(group(2))
            if slot == 9:
                arrive(3)
                emit(group(3))
        for act, h, lag in sides.get(slot, ()):
            if h < parts:
                each_lag(act, h, lag)
        if slot in points:
            point(points[slot])

    def ready(b):
        if b == 0:
            next(rest)
            point(3)
            if parts > 2:
                spread(2)
                side_start(2)
                emit(own(2))
            next(rest)
            if parts > 2:
                spread(3)
                side_start(3)
                emit(own(3))
            point(4)
            next(rest)
            point(5)
            for index, (i, j) in enumerate(pair_blocks(size)[1:]):
                place_block(i, j, full1[index * BLK : (index + 1) * BLK, :])
            innov_ref[...] = jnp.zeros((8, BLK), jnp.float32)
            for i in range(size // BLK):
                lane = i * BLK % width
                line = value_row + i * BLK // width
                value = pack_ref[line : line + 1, lane : lane + BLK]
                innov_ref[i : i + 1, :] = value - full1[place + i : place + i + 1, :]

    factor_inverse(mat, work, hook, ready)
    done = [16]

    def advance(last):
        while done[0] <= last:
            point(done[0])
            done[0] += 1

    advance(16)
    middle = size // 2
    across, along = (((1,), (1,)), ((), ())), (((1,), (0,)), ((), ()))
    high_w, low_w = split(mat[:, size:])

    def product(value, rows_w, lanes_w, dims):
        a, b = split(value)
        c, d = high_w[rows_w, lanes_w], low_w[rows_w, lanes_w]
        return matmul(a, c, dims) + matmul(a, d, dims) + matmul(b, c, dims)

    lower, upper, every = slice(0, middle), slice(middle, size), slice(0, size)
    step = rows // UNITS
    results = []
    for c in range(UNITS):
        where = slice(c * step, (c + 1) * step)
        gain_left = product(xr_ref[where, lower], lower, lower, across)
        gain_right = product(xr_ref[where, :], upper, every, across)
        u_ref[where, lower] = product(jnp.concatenate([gain_left, gain_right], axis=1), every, lower, along)
        u_ref[where, upper] = product(gain_right, upper, upper, along)
        results.append(pltpu.make_async_copy(u_ref.at[pl.ds(c * step, step)], u_out.at[pl.ds(c * step, step)], keep_sem.at[1]))
        results[-1].start()
        advance(done[0])
    for h in range(parts):
        side_take(h)
    advance(pieces + 3)
    pltpu.make_async_copy(u_ref, u_out, keep_sem.at[1]).wait()
    everything = pl.ds(0, rows)

    @pl.when(source)
    def _():
        pltpu.make_async_copy(xr_ref, xc_ref.at[low], keep_sem.at[0]).wait()

    for h in range(parts):
        plane[h][1][3].wait_send()
    _, _, sibs = onward(everything, xr_ref, 0)
    fewer = pl.ds(0, rows - rows // nc)
    up, down, _ = onward(fewer, xr_ref.at[fewer], 0)

    @pl.when(goes_up)
    def _():
        up.wait_send()

    @pl.when(goes_down)
    def _():
        down.wait_send()

    for sib in sibs:
        sib.wait()
    side_drain()


def padded(count, unit):
    return -(-count // unit) * unit


def exchange(mesh, covariance, pack, batches, foot):
    nr, nc = mesh.shape["row"], mesh.shape["col"]
    ratio = nr // nc
    rows, cols = covariance.shape
    size = batches * pack.shape[1]
    parts = part_count(rows, nc)
    group = ratio * nc
    lead = padded(BLK, 8 * group)
    follow = padded((len(pair_blocks(size)) - 1) * BLK + 8, 8 * group * nc)
    half, quarter = follow // ratio, follow // group
    land0 = (ratio - 1) * (lead // ratio) + 2 * (nc - 1) * (lead // group)
    land1 = (ratio - 1) * half + (nc - 1) * quarter + (nc - 1) * (quarter // nc)
    tall, flat = plane_shape(nc)
    sub = rows // (parts * nc)
    pieces = nc * parts
    sems = 2 * 2 * 3 + 4 * parts + pieces + ratio + 1 + nc * parts + 2 * nc
    f32 = jnp.float32
    vmem = pl.BlockSpec(memory_space=pltpu.VMEM)
    return pl.pallas_call(
        functools.partial(kernel, nr, nc, parts, batches, foot),
        out_shape=(
            jax.ShapeDtypeStruct((rows, size), f32),
            jax.ShapeDtypeStruct((ratio, rows, size), f32),
            jax.ShapeDtypeStruct((8, BLK), f32),
        ),
        in_specs=[pl.BlockSpec(memory_space=pl.ANY), vmem],
        out_specs=(pl.BlockSpec(memory_space=pl.ANY),) * 2 + (vmem,),
        scratch_shapes=[
            pltpu.VMEM((rows, size), f32),
            pltpu.SemaphoreType.DMA((2,)),
            pltpu.VMEM((rows, cols), f32),
            pltpu.VMEM((cols, size), jnp.bfloat16),
            pltpu.VMEM((cols, size), jnp.bfloat16),
            pltpu.VMEM((rows, size), f32),
            pltpu.VMEM((rows, size), f32),
            pltpu.VMEM((rows, size), f32),
            pltpu.VMEM((lead, BLK), f32),
            pltpu.VMEM((lead, BLK), f32),
            pltpu.VMEM((land0, BLK), f32),
            pltpu.VMEM((follow, BLK), f32),
            pltpu.VMEM((follow, BLK), f32),
            pltpu.VMEM((land1, BLK), f32),
            pltpu.VMEM((nc, parts * sub, size), f32),
            pltpu.VMEM((max((flat - 1) * tall, parts) * sub, size), f32),
            pltpu.VMEM((parts, flat - 1, tall, sub, size // 2), f32),
            pltpu.VMEM((parts, tall - 1, flat, sub, size // 2), f32),
            pltpu.VMEM((parts, tall, sub, size // 2), f32),
            pltpu.VMEM((parts, flat, sub, size // 2), f32),
            pltpu.VMEM((parts, tall - 1, sub, size // 2), f32),
            pltpu.VMEM((parts, flat - 1, sub, size // 2), f32),
            pltpu.VMEM((size, 2 * size), f32),
            pltpu.VMEM((BLK, 2 * BLK), f32),
            pltpu.SemaphoreType.DMA((sems,)),
            pltpu.SemaphoreType.DMA((sems,)),
            pltpu.SemaphoreType.DMA((parts,)),
        ],
        compiler_params=pltpu.CompilerParams(collective_id=0, has_side_effects=True, vmem_limit_bytes=40 * 1024 * 1024),
    )(covariance, pack)


def on_device(mesh, covariance, state_mean, obs_values, obs_cells, obs_weights, obs_variance):
    rows_dev, cols_dev = covariance.shape
    batches, foot, width = obs_cells.shape
    total = batches * width
    pack = jnp.concatenate(
        [
            obs_cells.astype(jnp.float32).reshape(batches * foot, width),
            obs_weights.reshape(batches * foot, width),
            obs_variance,
            obs_values,
            state_mean.reshape(rows_dev // width, width),
        ],
        axis=0,
    )
    u, cross_cols, innov = exchange(mesh, covariance, pack, batches, foot)
    innov = innov[: total // BLK].reshape(total)
    mean = state_mean + jnp.sum(u * innov[None, :], axis=1)
    update = jnp.dot(u, cross_cols.reshape(cols_dev, total).T, precision=MID, preferred_element_type=jnp.float32)
    return (covariance - update, mean)


def solution(mesh):
    return jax.shard_map(
        functools.partial(on_device, mesh),
        mesh=mesh,
        in_specs=(P("row", "col"), P("row"), P(), P(), P(), P()),
        out_specs=(P("row", "col"), P("row")),
        check_vma=False,
    )
```

```python
import functools

import jax
import jax.numpy as jnp
from jax import lax
from jax.experimental import pallas as pl
from jax.experimental.pallas import tpu as pltpu
from jax.sharding import PartitionSpec as P

HI = lax.Precision.HIGHEST
MID = lax.Precision.HIGH
MESH = pl.DeviceIdType.MESH
BLK = 128
SUB = 8
PANEL = 32
UNITS = 2

def base_inverse(work, hook):
    tiles = PANEL // SUB

    def panel_step(first, g, carry):
        start = pl.multiple_of(g * PANEL, PANEL)
        panel = work[pl.ds(start, PANEL), :]
        square = pltpu.roll(panel[:, :BLK], BLK - start, 1)[:, :PANEL]
        rows = [slice(t * SUB, (t + 1) * SUB) for t in range(tiles)]
        wide = [[jnp.broadcast_to(square[rows[t], j : j + 1], (SUB, BLK)) for t in range(tiles)] for j in range(PANEL)]
        left = [panel[rows[t], :BLK] for t in range(tiles)]
        right = [panel[rows[t], BLK:] for t in range(tiles)]
        below = lax.broadcasted_iota(jnp.int32, (SUB, BLK), 0)
        scale = [jnp.zeros((SUB, BLK), jnp.float32) for t in range(tiles)]
        for j in range(PANEL):
            home, at = j // SUB, j % SUB
            line = slice(at, at + 1)
            pivot = jnp.broadcast_to(wide[j][home][line, :], (SUB, BLK))
            root = lax.rsqrt(pivot)
            scale[home] = jnp.where(below == at, root, scale[home])
            pivot_left, pivot_right = left[home][line, :], right[home][line, :]
            pivot_wide = [wide[k][home][line, :] for k in range(PANEL)]
            for t in range(home, tiles):
                ratio = wide[j][t] * (1.0 / pivot)
                if t == home:
                    ratio = jnp.where(below > at, ratio, 0.0)
                left[t] = left[t] - ratio * pivot_left
                right[t] = right[t] - ratio * pivot_right
                for k in range(j + 1, PANEL):
                    wide[k][t] = wide[k][t] - ratio * pivot_wide[k]
        left = jnp.concatenate([left[t] * scale[t] for t in range(tiles)], axis=0)
        right = jnp.concatenate([right[t] * scale[t] for t in range(tiles)], axis=0)
        both = jnp.concatenate([left, right], axis=1)
        lane = lax.broadcasted_iota(jnp.int32, (PANEL, BLK), 1)
        lhs = jnp.where(lane >= start + PANEL, left, 0.0)
        work[pl.ds(start, PANEL), :] = both
        work[first:, :] = work[first:, :] - lax.dot_general(lhs[:, first:], both, (((0,), (0,)), ((), ())), precision=HI, preferred_element_type=jnp.float32)
        return carry

    steps = BLK // PANEL // 4
    for quarter in range(4):
        hook(quarter)
        first = quarter * steps * PANEL
        lax.fori_loop(quarter * steps, (quarter + 1) * steps, functools.partial(panel_step, first), 0)


def factor_inverse(mat, work, hook, ready):
    size = mat.shape[0]
    eye = (lax.broadcasted_iota(jnp.int32, (BLK, BLK), 0) == lax.broadcasted_iota(jnp.int32, (BLK, BLK), 1)).astype(jnp.float32)
    for b in range(size // BLK):
        lo, hi = b * BLK, (b + 1) * BLK
        work[:, :BLK] = mat[lo:hi, lo:hi]
        work[:, BLK:] = eye
        base_inverse(work, lambda quarter: hook(4 * b + quarter))
        winv = work[:, BLK:]
        ready(b)
        if hi < size:
            panel = jnp.dot(winv, mat[lo:hi, hi:size], precision=MID, preferred_element_type=jnp.float32)
        if lo > 0:
            left = jnp.dot(winv, mat[lo:hi, size : size + lo], precision=MID, preferred_element_type=jnp.float32)
            mat[lo:hi, size : size + lo] = left
        mat[lo:hi, size + lo : size + hi] = winv
        if hi < size:
            right = mat[lo:hi, size : size + hi]
            dims = (((0,), (0,)), ((), ()))
            mat[hi:size, hi:size] = mat[hi:size, hi:size] - lax.dot_general(panel, panel, dims, precision=MID, preferred_element_type=jnp.float32)
            mat[hi:size, size : size + hi] = mat[hi:size, size : size + hi] - lax.dot_general(panel, right, dims, precision=MID, preferred_element_type=jnp.float32)


def pair_blocks(size):
    count = size // BLK
    return [(i, j) for i in range(count) for j in range(i + 1)]


def split(value):
    high = value.astype(jnp.bfloat16)
    return high, (value - high.astype(jnp.float32)).astype(jnp.bfloat16)


def matmul(a, b, dims=(((1,), (0,)), ((), ()))):
    return lax.dot_general(a, b, dims, preferred_element_type=jnp.float32)


def part_count(rows, nc):
    return 4 if rows % (4 * nc * SUB) == 0 else 2


def plane_shape(nc):
    flat = max(d for d in range(1, nc + 1) if nc % d == 0 and d * d <= nc)
    return nc // flat, flat


def relay_order(nc, parts):
    order = []
    for pair in range(0, parts, 2):
        order += [(0, pair), (0, pair + 1)]
        order += [(d, h) for h in (pair, pair + 1) for d in range(1, nc)]
    return order


def kernel(
    nr, nc, parts, batches, foot, p_ref, pack_ref, u_out, xc_ref, innov_ref,
    u_ref, keep_sem, block, high_op, low_op, row_op, t_ref, xr_ref, acc0, full0, land0, acc1, full1, land1,
    side_ref, tland, land_a, land_b, mid_a, mid_b, next_a, next_b, mat, work, send_sem, recv_sem, load_sem,
):
    ratio = nr // nc
    row, col = lax.axis_index("row"), lax.axis_index("col")
    high, low = row // ratio, row % ratio
    rows, size = t_ref.shape
    wide = block.shape[1]
    part = rows // parts
    sub = part // nc
    order = relay_order(nc, parts)
    pieces = len(order)
    used = [0]

    def take(count):
        used[0] += count
        return used[0] - count

    width = pack_ref.shape[1]
    listed = batches * foot
    var_row, value_row, state_row = 2 * listed, 2 * listed + batches, 2 * listed + 2 * batches
    loads = []
    for h in range(parts):
        where = pl.ds(h * part, part)
        loads.append(pltpu.make_async_copy(p_ref.at[where], block.at[where], load_sem.at[h]))
        loads[-1].start()

    levels = [
        (ratio, low, lambda d: (high * ratio + lax.rem(low + d, ratio), col)),
        (nc, col, lambda d: (row, lax.rem(col + d, nc))),
        (nc, high, lambda d: (lax.rem(high + d, nc) * ratio + low, col)),
    ]
    barrier = pltpu.get_barrier_semaphore()
    for n, me, peer in levels:
        for d in range(1, n):
            pl.semaphore_signal(barrier, inc=1, device_id=peer(d), device_id_type=MESH)

    def operator(first, count, store):
        step = min(count, BLK)

        def fill(g, carry):
            start = pl.multiple_of(g * step, step)
            place = (lax.broadcasted_iota(jnp.int32, (step, width), 0) + (first + start)).astype(jnp.float32)
            for b in range(batches):
                total = jnp.zeros((step, width), jnp.float32)
                for f in range(foot):
                    at = b * foot + f
                    weight = pack_ref[listed + at : listed + at + 1, :]
                    total = total + jnp.where(pack_ref[at : at + 1, :] == place, weight, 0.0)
                store(start, step, b * width, width, total)
            return carry

        lax.fori_loop(0, count // step, fill, 0)

    def store_col(start, step, lane, width, total):
        h, l = split(total)
        high_op[pl.ds(start, step), lane : lane + width] = h
        low_op[pl.ds(start, step), lane : lane + width] = l

    def store_row(start, step, lane, width, total):
        row_op[pl.ds(start, step), lane : lane + width] = total

    operator(col * wide, wide, store_col)

    def remote(src, dst, sem, device):
        return pltpu.make_async_remote_copy(
            src_ref=src, dst_ref=dst, send_sem=send_sem.at[sem], recv_sem=recv_sem.at[sem],
            device_id=device, device_id_type=MESH,
        )

    def own_rows(h, owner):
        return pl.ds(pl.multiple_of(h * part + owner * sub, 8), sub)

    _, _, col_peer = levels[1]
    _, _, low_peer = levels[0]
    tall, flat = plane_shape(nc)
    hi, lo = col // flat, col % flat
    half = size // 2
    left, right = pl.ds(0, half), pl.ds(half, half)
    chain_base = send_sem.shape[0]
    sib_base = take(ratio - 1)
    up_sem, down_sem = sib_base + ratio - 1, sib_base + ratio
    take(2)

    def lo_peer(d):
        return (row, hi * flat + lax.rem(lo + d, flat))

    def hi_peer(d):
        return (row, lax.rem(hi + d, tall) * flat + lo)

    def plane_copies(h):
        stages = scatter, settle, spread, pass_on = [], [], [], []
        base = take(len(stages))

        def add(group, src, dst, device):
            stage = [n for n in range(len(stages)) if stages[n] is group][0]
            group.append(remote(src, dst, base + stage, device))

        own = own_rows(h, col)
        for d in range(1, flat):
            other = lax.rem(lo + d, flat)
            for k in range(tall):
                add(scatter, t_ref.at[own_rows(h, k * flat + other), left], land_a.at[h, d - 1, k], lo_peer(d))
            add(settle, mid_b.at[h, other], next_b.at[h, d - 1], lo_peer(d))
            add(spread, xr_ref.at[own, left], xr_ref.at[own, left], lo_peer(d))
            for k in range(tall):
                where = own_rows(h, k * flat + lo)
                add(pass_on, xr_ref.at[where, right], xr_ref.at[where, right], lo_peer(d))
        for d in range(1, tall):
            other = lax.rem(hi + d, tall)
            for k in range(flat):
                add(scatter, t_ref.at[own_rows(h, other * flat + k), right], land_b.at[h, d - 1, k], hi_peer(d))
            add(settle, mid_a.at[h, other], next_a.at[h, d - 1], hi_peer(d))
            add(spread, xr_ref.at[own, right], xr_ref.at[own, right], hi_peer(d))
            for k in range(flat):
                where = own_rows(h, hi * flat + k)
                add(pass_on, xr_ref.at[where, left], xr_ref.at[where, left], hi_peer(d))
        near = (flat - 1) + (tall - 1)
        wide_count = (flat - 1) * tall + (tall - 1) * flat
        ends = []
        for stage, count in enumerate((wide_count, near, near, wide_count)):
            every = tland.at[pl.ds(0, count * sub // 2)]
            ends.append(remote(every, every, base + stage, lo_peer(1)))
        return stages, ends

    plane = [plane_copies(h) for h in range(parts)]

    def start_all(copies):
        for copy in copies:
            copy.start()

    def scatter(h):
        start_all(plane[h][0][0])

    def settle(h):
        plane[h][1][0].wait()
        for k in range(tall):
            total = t_ref[own_rows(h, k * flat + lo), left]
            for d in range(1, flat):
                total = total + land_a[h, d - 1, k]
            mid_a[h, k] = total
        for k in range(flat):
            total = t_ref[own_rows(h, hi * flat + k), right]
            for d in range(1, tall):
                total = total + land_b[h, d - 1, k]
            mid_b[h, k] = total
        start_all(plane[h][0][1])

    def spread(h):
        plane[h][1][1].wait()
        total = mid_a[h, hi]
        for d in range(1, tall):
            total = total + next_a[h, d - 1]
        xr_ref[own_rows(h, col), left] = total
        total = mid_b[h, lo]
        for d in range(1, flat):
            total = total + next_b[h, d - 1]
        xr_ref[own_rows(h, col), right] = total
        start_all(plane[h][0][2])

    def pass_on(h):
        plane[h][1][2].wait()
        start_all(plane[h][0][3])

    def arrive(h):
        plane[h][1][3].wait_recv()

    source = high == col
    far = jnp.abs(high - col)
    top = nc - 1
    above = (jnp.minimum(high + 1, top) * ratio + low, col)
    below = (jnp.maximum(high - 1, 0) * ratio + low, col)
    goes_up = jnp.logical_and(high >= col, high < top)
    goes_down = jnp.logical_and(high <= col, high > 0)

    def onward(where, src, e):
        dst = xc_ref.at[low, where]
        up = pltpu.make_async_remote_copy(
            src_ref=src, dst_ref=dst, send_sem=send_sem.at[up_sem], recv_sem=recv_sem.at[chain_base + e],
            device_id=above, device_id_type=MESH,
        )
        down = pltpu.make_async_remote_copy(
            src_ref=src, dst_ref=dst, send_sem=send_sem.at[down_sem], recv_sem=recv_sem.at[chain_base + e],
            device_id=below, device_id_type=MESH,
        )
        sibs = [remote(src, dst, sib_base + q - 1, low_peer(q)) for q in range(1, ratio)]
        return up, down, sibs

    def links(e, src_is_own):
        d, h = order[e]
        where = own_rows(h, lax.rem(col - d + nc, nc))
        src = xr_ref.at[where] if src_is_own else xc_ref.at[low, where]
        return (where,) + onward(where, src, e)

    def send_on(e, up, down, sibs):
        owner = lax.rem(col - order[e][0] + nc, nc)

        @pl.when(jnp.logical_and(goes_up, owner != top))
        def _():
            up.start()

        @pl.when(jnp.logical_and(goes_down, owner != 0))
        def _():
            down.start()

        for sib in sibs:
            sib.start()

    def keep(e):
        d, h = order[e]
        where = own_rows(h, lax.rem(col - d + nc, nc))
        return pltpu.make_async_copy(xr_ref.at[where], xc_ref.at[low, where], keep_sem.at[0])

    def relay_source(e):
        d, h = order[e]
        where, up, down, sibs = links(e, True)
        send_on(e, up, down, sibs)
        keep(e).start()

    def relay(e):
        where, up, down, sibs = links(e, False)
        up.wait_recv()
        send_on(e, up, down, sibs)

    side_recv = chain_base + pieces
    side_send = take(2 * nc)
    last_up = jnp.logical_and(col == top, high < top)
    last_down = jnp.logical_and(col == 0, high > 0)

    def side(src, slot, h, lag, device):
        dst = side_ref.at[slot, pl.ds(h * sub, sub)]
        return pltpu.make_async_remote_copy(
            src_ref=src, dst_ref=dst, send_sem=send_sem.at[side_send + lag],
            recv_sem=recv_sem.at[side_recv + slot * parts + h], device_id=device, device_id_type=MESH,
        )

    def deliver(slot, h, lag, upward):
        first = (h // 2) * 2 * nc + 2 + (h % 2) * (nc - 1)
        e = first + (slot if upward else slot - 1)
        return pltpu.make_async_remote_copy(
            src_ref=side_ref.at[slot, pl.ds(h * sub, sub)], dst_ref=xc_ref.at[low, own_rows(h, top if upward else 0)],
            send_sem=send_sem.at[side_send + nc + lag], recv_sem=recv_sem.at[chain_base + e],
            device_id=(row, slot), device_id_type=MESH,
        )

    def side_start(h):
        for test, device in ((last_up, above), (last_down, below)):
            @pl.when(test)
            def _():
                side(xr_ref.at[own_rows(h, col)], high, h, 0, device).start()

    def side_edges(lag):
        up, down = high - lag, high + lag
        return (
            (True, up, jnp.logical_and(col == top, up >= 0), above, high < top),
            (False, down, jnp.logical_and(col == 0, down <= top), below, high > 0),
        )

    def side_forward(h, lag):
        for _, slot, edge, device, onward_too in side_edges(lag):
            @pl.when(edge)
            def _():
                copy = side(side_ref.at[slot, pl.ds(h * sub, sub)], slot, h, lag, device)
                copy.wait_recv()
                pl.when(onward_too)(copy.start)

    def side_deliver(h, lag):
        for upward, slot, edge, _, _ in side_edges(lag):
            pl.when(edge)(deliver(slot, h, lag, upward).start)

    def each_lag(act, h, lag):
        for each in range(lag, nc if lag == 3 else min(lag + 1, nc)):
            act(h, each)

    def side_take(h):
        @pl.when(jnp.logical_not(source))
        def _():
            e = (h // 2) * 2 * nc + 2 + (h % 2) * (nc - 1) + jnp.where(high > col, col, col - 1)
            where = own_rows(h, jnp.where(high > col, top, 0))
            up, _, sibs = onward(where, xc_ref.at[low, where], e)
            up.wait_recv()
            for sib in sibs:
                sib.start()

    def side_drain():
        span = pl.ds(0, parts * sub)
        for upward in (True, False):
            for lag in range(nc):
                slot = high - lag if upward else high + lag
                edge = jnp.logical_and(col == top, slot >= 0) if upward else jnp.logical_and(col == 0, slot <= top)
                whole = pltpu.make_async_remote_copy(
                    src_ref=tland.at[span], dst_ref=tland.at[span], send_sem=send_sem.at[side_send + lag],
                    recv_sem=recv_sem.at[side_recv], device_id=above, device_id_type=MESH,
                )
                pl.when(jnp.logical_and(edge, high < top if upward else high > 0))(whole.wait_send)
                if lag > 0:
                    whole = pltpu.make_async_remote_copy(
                        src_ref=tland.at[span], dst_ref=tland.at[span], send_sem=send_sem.at[side_send + nc + lag],
                        recv_sem=recv_sem.at[side_recv], device_id=above, device_id_type=MESH,
                    )
                    pl.when(edge)(whole.wait_send)

    def emit(pieces_now):
        @pl.when(source)
        def _():
            for e in pieces_now:
                relay_source(e)

    def group(h):
        return [e for e in range(pieces) if order[e][1] == h and order[e][0] > 0]

    def own(h):
        return [order.index((0, h))]

    def point(k):
        for test, lag in ((far == 1, 0), (far == 2, 2), (far > 2, 4)):
            if 0 <= k - lag < pieces:
                owner = lax.rem(col - order[k - lag][0] + nc, nc)
                chained = owner != jnp.where(high > col, top, 0)
                pl.when(jnp.logical_and(test, chained))(functools.partial(relay, k - lag))

    for h in range(parts):
        loads[h].wait()
        where = slice(h * part, (h + 1) * part)
        a, b = split(block[where, :])
        t_ref[where, :] = matmul(a, high_op[...]) + matmul(a, low_op[...]) + matmul(b, high_op[...])
        if h == 0:
            pl.semaphore_wait(barrier, ratio - 1 + 2 * (nc - 1))
        if h < 2:
            scatter(h)
        if h == parts - 2:
            operator(row * rows, rows, store_row)

    def reduced(acc, full, land, spread):
        start, length, slot = 0, acc.shape[0], 0
        spots = []

        def exchange_all(level, pairs, count):
            n, me, peer = levels[level]
            base = take(1)
            for d in range(1, n):
                src, dst = pairs(d)
                remote(src, dst, base, peer(d)).start()
            every = land.at[pl.ds(0, (n - 1) * count)]
            return remote(every, every, base, peer(1))

        for level, (n, me, peer) in enumerate(levels):
            whole = level == 2 and not spread
            segment = length if whole else length // n

            def scattered(d):
                begin = start if whole else pl.multiple_of(start + lax.rem(me + d, n) * segment, 8)
                return acc.at[pl.ds(begin, segment)], land.at[pl.ds(slot + (d - 1) * segment, segment)]

            end = exchange_all(level, scattered, segment)
            yield
            if not whole:
                start = pl.multiple_of(start + me * segment, 8)
                spots.append((start, segment))
            length = segment
            end.wait()
            where = pl.ds(start, length)
            mine = acc[where, :]
            for d in range(1, n):
                mine = mine + land[pl.ds(slot + (d - 1) * segment, segment), :]
            slot += (n - 1) * segment
            if level == 2:
                full[where, :] = mine
            else:
                acc[where, :] = mine
        for level in (2, 1, 0) if spread else (1, 0):
            begin, segment = spots[level]
            where = full.at[pl.ds(begin, segment)]
            end = exchange_all(level, lambda d: (where, where), segment)
            yield
            end.wait()
        yield

    def sums(i):
        return lax.dot_general(
            row_op[:, i * BLK : (i + 1) * BLK], t_ref[:, : (i + 1) * BLK], (((0,), (0,)), ((), ())),
            precision=MID, preferred_element_type=jnp.float32,
        )

    first = reduced(acc0, full0, land0, False)
    rest = reduced(acc1, full1, land1, True)
    place = 0
    settle(0)
    for i in range(size // BLK):
        blocks = sums(i)
        if i == 0:
            acc0[:BLK, :] = blocks
            if acc0.shape[0] > BLK:
                acc0[BLK:, :] = jnp.zeros((acc0.shape[0] - BLK, BLK), jnp.float32)
            next(first)
            continue
        for j in range(i + 1):
            acc1[place : place + BLK, :] = blocks[:, j * BLK : (j + 1) * BLK]
            place += BLK
        if i == 1:
            next(first)
            settle(1)
        if i == 2:
            spread(0)
            next(first)
            emit(own(0))
            side_start(0)
    predicted = jnp.zeros((1, size), jnp.float32)
    for q in range(rows // width):
        state = pack_ref[state_row + q : state_row + q + 1, :]
        predicted = predicted + jnp.dot(
            state, row_op[q * width : (q + 1) * width, :], precision=HI, preferred_element_type=jnp.float32
        )
    predicted = jnp.where(col == 0, predicted, 0.0)
    acc1[place:, :] = jnp.zeros((acc1.shape[0] - place, BLK), jnp.float32)
    for i in range(size // BLK):
        acc1[place + i : place + i + 1, :] = predicted[:, i * BLK : (i + 1) * BLK]
    next(rest)
    spread(1)
    side_start(1)
    pass_on(0)
    emit(own(1))
    next(first)
    next(rest)
    pass_on(1)
    next(first)
    point(0)
    next(first)
    next(rest)
    arrive(0)
    emit(group(0)[:1])
    if parts > 2:
        scatter(2)
        scatter(3)
    point(1)

    same = lax.broadcasted_iota(jnp.int32, (BLK, BLK), 0) == lax.broadcasted_iota(jnp.int32, (BLK, BLK), 1)

    def place_block(i, j, square):
        if i == j:
            lane = i * BLK % width
            line = var_row + i * BLK // width
            diagonal = pack_ref[line : line + 1, lane : lane + BLK]
            square = 0.5 * (square + square.T) + jnp.where(same, diagonal, 0.0)
        mat[i * BLK : (i + 1) * BLK, j * BLK : (j + 1) * BLK] = square
        if i != j:
            mat[j * BLK : (j + 1) * BLK, i * BLK : (i + 1) * BLK] = square.T

    place_block(0, 0, full0[:BLK, :])
    mat[:, size:] = jnp.zeros((size, size), jnp.float32)

    points = {2: 2, 4: 6, 5: 7, 6: 8, 7: 9, 8: 10, 10: 11, 11: 12, 12: 13, 13: 14, 15: 15}

    sides = {
        4: [(side_forward, 0, 2), (side_forward, 1, 2)],
        6: [(side_forward, 2, 1), (side_deliver, 0, 1), (side_deliver, 1, 1)],
        7: [(side_forward, 3, 1)],
        8: [(side_deliver, 0, 2), (side_deliver, 1, 2), (side_forward, 0, 3), (side_forward, 1, 3), (side_deliver, 0, 3), (side_deliver, 1, 3)],
        9: [(side_forward, 2, 2), (side_deliver, 2, 1), (side_deliver, 3, 1)],
        11: [(side_forward, 3, 2)],
        12: [(side_deliver, 2, 2), (side_deliver, 3, 2)],
        14: [(side_forward, 2, 3), (side_deliver, 2, 3)],
        15: [(side_forward, 3, 3), (side_deliver, 3, 3)],
    }

    def hook(slot):
        if slot == 1:
            next(rest)
            emit(group(0)[1:])
            for h in range(2):
                each_lag(side_forward, h, 1)
        if parts > 2 and slot == 2:
            settle(2)
        if slot == 3:
            next(rest)
            arrive(1)
            emit(group(1))
        if parts > 2:
            if slot == 3:
                settle(3)
            if slot == 4:
                pass_on(2)
            if slot == 5:
                pass_on(3)
            if slot == 7:
                arrive(2)
                emit(group(2))
            if slot == 9:
                arrive(3)
                emit(group(3))
        for act, h, lag in sides.get(slot, ()):
            if h < parts:
                each_lag(act, h, lag)
        if slot in points:
            point(points[slot])

    def ready(b):
        if b == 0:
            point(3)
            if parts > 2:
                spread(2)
                side_start(2)
                emit(own(2))
            next(rest)
            if parts > 2:
                spread(3)
                side_start(3)
                emit(own(3))
            point(4)
            next(rest)
            point(5)
            for index, (i, j) in enumerate(pair_blocks(size)[1:]):
                place_block(i, j, full1[index * BLK : (index + 1) * BLK, :])
            innov_ref[...] = jnp.zeros((8, BLK), jnp.float32)
            for i in range(size // BLK):
                lane = i * BLK % width
                line = value_row + i * BLK // width
                value = pack_ref[line : line + 1, lane : lane + BLK]
                innov_ref[i : i + 1, :] = value - full1[place + i : place + i + 1, :]

    factor_inverse(mat, work, hook, ready)
    done = [16]

    def advance(last):
        while done[0] <= last:
            point(done[0])
            done[0] += 1

    advance(16)
    middle = size // 2
    across, along = (((1,), (1,)), ((), ())), (((1,), (0,)), ((), ()))
    high_w, low_w = split(mat[:, size:])

    def product(value, rows_w, lanes_w, dims):
        a, b = split(value)
        c, d = high_w[rows_w, lanes_w], low_w[rows_w, lanes_w]
        return matmul(a, c, dims) + matmul(a, d, dims) + matmul(b, c, dims)

    lower, upper, every = slice(0, middle), slice(middle, size), slice(0, size)
    step = rows // UNITS
    results = []
    for c in range(UNITS):
        where = slice(c * step, (c + 1) * step)
        gain_left = product(xr_ref[where, lower], lower, lower, across)
        gain_right = product(xr_ref[where, :], upper, every, across)
        u_ref[where, lower] = product(jnp.concatenate([gain_left, gain_right], axis=1), every, lower, along)
        u_ref[where, upper] = product(gain_right, upper, upper, along)
        results.append(pltpu.make_async_copy(u_ref.at[pl.ds(c * step, step)], u_out.at[pl.ds(c * step, step)], keep_sem.at[1]))
        results[-1].start()
        advance(done[0])
    for h in range(parts):
        side_take(h)
    advance(pieces + 3)
    pltpu.make_async_copy(u_ref, u_out, keep_sem.at[1]).wait()
    everything = pl.ds(0, rows)

    @pl.when(source)
    def _():
        pltpu.make_async_copy(xr_ref, xc_ref.at[low], keep_sem.at[0]).wait()

    for h in range(parts):
        plane[h][1][3].wait_send()
    _, _, sibs = onward(everything, xr_ref, 0)
    fewer = pl.ds(0, rows - rows // nc)
    up, down, _ = onward(fewer, xr_ref.at[fewer], 0)

    @pl.when(goes_up)
    def _():
        up.wait_send()

    @pl.when(goes_down)
    def _():
        down.wait_send()

    for sib in sibs:
        sib.wait()
    side_drain()


def padded(count, unit):
    return -(-count // unit) * unit


def exchange(mesh, covariance, pack, batches, foot):
    nr, nc = mesh.shape["row"], mesh.shape["col"]
    ratio = nr // nc
    rows, cols = covariance.shape
    size = batches * pack.shape[1]
    parts = part_count(rows, nc)
    group = ratio * nc
    lead = padded(BLK, 8 * group)
    follow = padded((len(pair_blocks(size)) - 1) * BLK + 8, 8 * group * nc)
    half, quarter = follow // ratio, follow // group
    land0 = (ratio - 1) * (lead // ratio) + 2 * (nc - 1) * (lead // group)
    land1 = (ratio - 1) * half + (nc - 1) * quarter + (nc - 1) * (quarter // nc)
    tall, flat = plane_shape(nc)
    sub = rows // (parts * nc)
    pieces = nc * parts
    sends = 2 * 2 * 3 - 1 + 4 * parts + ratio + 1 + 2 * nc
    receives = sends + pieces + nc * parts
    f32 = jnp.float32
    vmem = pl.BlockSpec(memory_space=pltpu.VMEM)
    return pl.pallas_call(
        functools.partial(kernel, nr, nc, parts, batches, foot),
        out_shape=(
            jax.ShapeDtypeStruct((rows, size), f32),
            jax.ShapeDtypeStruct((ratio, rows, size), f32),
            jax.ShapeDtypeStruct((8, BLK), f32),
        ),
        in_specs=[pl.BlockSpec(memory_space=pl.ANY), vmem],
        out_specs=(pl.BlockSpec(memory_space=pl.ANY),) * 2 + (vmem,),
        scratch_shapes=[
            pltpu.VMEM((rows, size), f32),
            pltpu.SemaphoreType.DMA((2,)),
            pltpu.VMEM((rows, cols), f32),
            pltpu.VMEM((cols, size), jnp.bfloat16),
            pltpu.VMEM((cols, size), jnp.bfloat16),
            pltpu.VMEM((rows, size), f32),
            pltpu.VMEM((rows, size), f32),
            pltpu.VMEM((rows, size), f32),
            pltpu.VMEM((lead, BLK), f32),
            pltpu.VMEM((lead, BLK), f32),
            pltpu.VMEM((land0, BLK), f32),
            pltpu.VMEM((follow, BLK), f32),
            pltpu.VMEM((follow, BLK), f32),
            pltpu.VMEM((land1, BLK), f32),
            pltpu.VMEM((nc, parts * sub, size), f32),
            pltpu.VMEM((max((flat - 1) * tall, parts) * sub, size), f32),
            pltpu.VMEM((parts, flat - 1, tall, sub, size // 2), f32),
            pltpu.VMEM((parts, tall - 1, flat, sub, size // 2), f32),
            pltpu.VMEM((parts, tall, sub, size // 2), f32),
            pltpu.VMEM((parts, flat, sub, size // 2), f32),
            pltpu.VMEM((parts, tall - 1, sub, size // 2), f32),
            pltpu.VMEM((parts, flat - 1, sub, size // 2), f32),
            pltpu.VMEM((size, 2 * size), f32),
            pltpu.VMEM((BLK, 2 * BLK), f32),
            pltpu.SemaphoreType.DMA((sends,)),
            pltpu.SemaphoreType.DMA((receives,)),
            pltpu.SemaphoreType.DMA((parts,)),
        ],
        compiler_params=pltpu.CompilerParams(collective_id=0, has_side_effects=True, vmem_limit_bytes=40 * 1024 * 1024),
    )(covariance, pack)


def on_device(mesh, covariance, state_mean, obs_values, obs_cells, obs_weights, obs_variance):
    rows_dev, cols_dev = covariance.shape
    batches, foot, width = obs_cells.shape
    total = batches * width
    pack = jnp.concatenate(
        [
            obs_cells.astype(jnp.float32).reshape(batches * foot, width),
            obs_weights.reshape(batches * foot, width),
            obs_variance,
            obs_values,
            state_mean.reshape(rows_dev // width, width),
        ],
        axis=0,
    )
    u, cross_cols, innov = exchange(mesh, covariance, pack, batches, foot)
    innov = innov[: total // BLK].reshape(total)
    mean = state_mean + jnp.sum(u * innov[None, :], axis=1)
    update = jnp.dot(u, cross_cols.reshape(cols_dev, total).T, precision=MID, preferred_element_type=jnp.float32)
    return (covariance - update, mean)


def solution(mesh):
    return jax.shard_map(
        functools.partial(on_device, mesh),
        mesh=mesh,
        in_specs=(P("row", "col"), P("row"), P(), P(), P(), P()),
        out_specs=(P("row", "col"), P("row")),
        check_vma=False,
    )
```

```python
import functools

import jax
import jax.numpy as jnp
from jax import lax
from jax.experimental import pallas as pl
from jax.experimental.pallas import tpu as pltpu
from jax.sharding import PartitionSpec as P

HI = lax.Precision.HIGHEST
MID = lax.Precision.HIGH
MESH = pl.DeviceIdType.MESH
BLK = 128
SUB = 8
PANEL = 32
UNITS = 2

def base_inverse(work, hook):
    tiles = PANEL // SUB

    def panel_step(first, g, carry):
        start = pl.multiple_of(g * PANEL, PANEL)
        panel = work[pl.ds(start, PANEL), :]
        square = pltpu.roll(panel[:, :BLK], BLK - start, 1)[:, :PANEL]
        rows = [slice(t * SUB, (t + 1) * SUB) for t in range(tiles)]
        wide = [[jnp.broadcast_to(square[rows[t], j : j + 1], (SUB, BLK)) for t in range(tiles)] for j in range(PANEL)]
        left = [panel[rows[t], :BLK] for t in range(tiles)]
        right = [panel[rows[t], BLK:] for t in range(tiles)]
        below = lax.broadcasted_iota(jnp.int32, (SUB, BLK), 0)
        scale = [jnp.zeros((SUB, BLK), jnp.float32) for t in range(tiles)]
        for j in range(PANEL):
            home, at = j // SUB, j % SUB
            line = slice(at, at + 1)
            pivot = jnp.broadcast_to(wide[j][home][line, :], (SUB, BLK))
            root = lax.rsqrt(pivot)
            scale[home] = jnp.where(below == at, root, scale[home])
            pivot_left, pivot_right = left[home][line, :], right[home][line, :]
            pivot_wide = [wide[k][home][line, :] for k in range(PANEL)]
            for t in range(home, tiles):
                ratio = wide[j][t] * (1.0 / pivot)
                if t == home:
                    ratio = jnp.where(below > at, ratio, 0.0)
                left[t] = left[t] - ratio * pivot_left
                right[t] = right[t] - ratio * pivot_right
                for k in range(j + 1, PANEL):
                    wide[k][t] = wide[k][t] - ratio * pivot_wide[k]
        left = jnp.concatenate([left[t] * scale[t] for t in range(tiles)], axis=0)
        right = jnp.concatenate([right[t] * scale[t] for t in range(tiles)], axis=0)
        both = jnp.concatenate([left, right], axis=1)
        lane = lax.broadcasted_iota(jnp.int32, (PANEL, BLK), 1)
        lhs = jnp.where(lane >= start + PANEL, left, 0.0)
        work[pl.ds(start, PANEL), :] = both
        work[first:, :] = work[first:, :] - lax.dot_general(lhs[:, first:], both, (((0,), (0,)), ((), ())), precision=MID, preferred_element_type=jnp.float32)
        return carry

    steps = BLK // PANEL // 4
    for quarter in range(4):
        hook(quarter)
        first = quarter * steps * PANEL
        lax.fori_loop(quarter * steps, (quarter + 1) * steps, functools.partial(panel_step, first), 0)


def factor_inverse(mat, work, hook, ready):
    size = mat.shape[0]
    eye = (lax.broadcasted_iota(jnp.int32, (BLK, BLK), 0) == lax.broadcasted_iota(jnp.int32, (BLK, BLK), 1)).astype(jnp.float32)
    for b in range(size // BLK):
        lo, hi = b * BLK, (b + 1) * BLK
        work[:, :BLK] = mat[lo:hi, lo:hi]
        work[:, BLK:] = eye
        base_inverse(work, lambda quarter: hook(4 * b + quarter))
        winv = work[:, BLK:]
        ready(b)
        if hi < size:
            panel = jnp.dot(winv, mat[lo:hi, hi:size], precision=MID, preferred_element_type=jnp.float32)
        if lo > 0:
            left = jnp.dot(winv, mat[lo:hi, size : size + lo], precision=MID, preferred_element_type=jnp.float32)
            mat[lo:hi, size : size + lo] = left
        mat[lo:hi, size + lo : size + hi] = winv
        if hi < size:
            right = mat[lo:hi, size : size + hi]
            dims = (((0,), (0,)), ((), ()))
            mat[hi:size, hi:size] = mat[hi:size, hi:size] - lax.dot_general(panel, panel, dims, precision=MID, preferred_element_type=jnp.float32)
            mat[hi:size, size : size + hi] = mat[hi:size, size : size + hi] - lax.dot_general(panel, right, dims, precision=MID, preferred_element_type=jnp.float32)


def pair_blocks(size):
    count = size // BLK
    return [(i, j) for i in range(count) for j in range(i + 1)]


def split(value):
    high = value.astype(jnp.bfloat16)
    return high, (value - high.astype(jnp.float32)).astype(jnp.bfloat16)


def matmul(a, b, dims=(((1,), (0,)), ((), ()))):
    return lax.dot_general(a, b, dims, preferred_element_type=jnp.float32)


def part_count(rows, nc):
    return 4 if rows % (4 * nc * SUB) == 0 else 2


def plane_shape(nc):
    flat = max(d for d in range(1, nc + 1) if nc % d == 0 and d * d <= nc)
    return nc // flat, flat


def relay_order(nc, parts):
    order = []
    for pair in range(0, parts, 2):
        order += [(0, pair), (0, pair + 1)]
        order += [(d, h) for h in (pair, pair + 1) for d in range(1, nc)]
    return order


def kernel(
    nr, nc, parts, batches, foot, p_ref, pack_ref, u_out, xc_ref, innov_ref,
    u_ref, keep_sem, block, high_op, low_op, row_op, t_ref, xr_ref, acc0, full0, land0, acc1, full1, land1,
    side_ref, tland, land_a, land_b, mid_a, mid_b, next_a, next_b, mat, work, send_sem, recv_sem, load_sem,
):
    ratio = nr // nc
    row, col = lax.axis_index("row"), lax.axis_index("col")
    high, low = row // ratio, row % ratio
    rows, size = t_ref.shape
    wide = block.shape[1]
    part = rows // parts
    sub = part // nc
    order = relay_order(nc, parts)
    pieces = len(order)
    used = [0]

    def take(count):
        used[0] += count
        return used[0] - count

    width = pack_ref.shape[1]
    listed = batches * foot
    var_row, value_row, state_row = 2 * listed, 2 * listed + batches, 2 * listed + 2 * batches
    loads = []
    for h in range(parts):
        where = pl.ds(h * part, part)
        loads.append(pltpu.make_async_copy(p_ref.at[where], block.at[where], load_sem.at[h]))
        loads[-1].start()

    levels = [
        (ratio, low, lambda d: (high * ratio + lax.rem(low + d, ratio), col)),
        (nc, col, lambda d: (row, lax.rem(col + d, nc))),
        (nc, high, lambda d: (lax.rem(high + d, nc) * ratio + low, col)),
    ]
    barrier = pltpu.get_barrier_semaphore()
    for n, me, peer in levels:
        for d in range(1, n):
            pl.semaphore_signal(barrier, inc=1, device_id=peer(d), device_id_type=MESH)

    def operator(first, count, store):
        step = min(count, BLK)

        def fill(g, carry):
            start = pl.multiple_of(g * step, step)
            place = (lax.broadcasted_iota(jnp.int32, (step, width), 0) + (first + start)).astype(jnp.float32)
            for b in range(batches):
                total = jnp.zeros((step, width), jnp.float32)
                for f in range(foot):
                    at = b * foot + f
                    weight = pack_ref[listed + at : listed + at + 1, :]
                    total = total + jnp.where(pack_ref[at : at + 1, :] == place, weight, 0.0)
                store(start, step, b * width, width, total)
            return carry

        lax.fori_loop(0, count // step, fill, 0)

    def store_col(start, step, lane, width, total):
        h, l = split(total)
        high_op[pl.ds(start, step), lane : lane + width] = h
        low_op[pl.ds(start, step), lane : lane + width] = l

    def store_row(start, step, lane, width, total):
        row_op[pl.ds(start, step), lane : lane + width] = total

    operator(col * wide, wide, store_col)

    def remote(src, dst, sem, device):
        return pltpu.make_async_remote_copy(
            src_ref=src, dst_ref=dst, send_sem=send_sem.at[sem], recv_sem=recv_sem.at[sem],
            device_id=device, device_id_type=MESH,
        )

    def own_rows(h, owner):
        return pl.ds(pl.multiple_of(h * part + owner * sub, 8), sub)

    _, _, col_peer = levels[1]
    _, _, low_peer = levels[0]
    tall, flat = plane_shape(nc)
    hi, lo = col // flat, col % flat
    half = size // 2
    left, right = pl.ds(0, half), pl.ds(half, half)
    chain_base = send_sem.shape[0]
    sib_base = take(ratio - 1)
    up_sem, down_sem = sib_base + ratio - 1, sib_base + ratio
    take(2)

    def lo_peer(d):
        return (row, hi * flat + lax.rem(lo + d, flat))

    def hi_peer(d):
        return (row, lax.rem(hi + d, tall) * flat + lo)

    def plane_copies(h):
        stages = scatter, settle, spread, pass_on = [], [], [], []
        base = take(len(stages))

        def add(group, src, dst, device):
            stage = [n for n in range(len(stages)) if stages[n] is group][0]
            group.append(remote(src, dst, base + stage, device))

        own = own_rows(h, col)
        for d in range(1, flat):
            other = lax.rem(lo + d, flat)
            for k in range(tall):
                add(scatter, t_ref.at[own_rows(h, k * flat + other), left], land_a.at[h, d - 1, k], lo_peer(d))
            add(settle, mid_b.at[h, other], next_b.at[h, d - 1], lo_peer(d))
            add(spread, xr_ref.at[own, left], xr_ref.at[own, left], lo_peer(d))
            for k in range(tall):
                where = own_rows(h, k * flat + lo)
                add(pass_on, xr_ref.at[where, right], xr_ref.at[where, right], lo_peer(d))
        for d in range(1, tall):
            other = lax.rem(hi + d, tall)
            for k in range(flat):
                add(scatter, t_ref.at[own_rows(h, other * flat + k), right], land_b.at[h, d - 1, k], hi_peer(d))
            add(settle, mid_a.at[h, other], next_a.at[h, d - 1], hi_peer(d))
            add(spread, xr_ref.at[own, right], xr_ref.at[own, right], hi_peer(d))
            for k in range(flat):
                where = own_rows(h, hi * flat + k)
                add(pass_on, xr_ref.at[where, left], xr_ref.at[where, left], hi_peer(d))
        near = (flat - 1) + (tall - 1)
        wide_count = (flat - 1) * tall + (tall - 1) * flat
        ends = []
        for stage, count in enumerate((wide_count, near, near, wide_count)):
            every = tland.at[pl.ds(0, count * sub // 2)]
            ends.append(remote(every, every, base + stage, lo_peer(1)))
        return stages, ends

    plane = [plane_copies(h) for h in range(parts)]

    def start_all(copies):
        for copy in copies:
            copy.start()

    def scatter(h):
        start_all(plane[h][0][0])

    def settle(h):
        plane[h][1][0].wait()
        for k in range(tall):
            total = t_ref[own_rows(h, k * flat + lo), left]
            for d in range(1, flat):
                total = total + land_a[h, d - 1, k]
            mid_a[h, k] = total
        for k in range(flat):
            total = t_ref[own_rows(h, hi * flat + k), right]
            for d in range(1, tall):
                total = total + land_b[h, d - 1, k]
            mid_b[h, k] = total
        start_all(plane[h][0][1])

    def spread(h):
        plane[h][1][1].wait()
        total = mid_a[h, hi]
        for d in range(1, tall):
            total = total + next_a[h, d - 1]
        xr_ref[own_rows(h, col), left] = total
        total = mid_b[h, lo]
        for d in range(1, flat):
            total = total + next_b[h, d - 1]
        xr_ref[own_rows(h, col), right] = total
        start_all(plane[h][0][2])

    def pass_on(h):
        plane[h][1][2].wait()
        start_all(plane[h][0][3])

    def arrive(h):
        plane[h][1][3].wait_recv()

    source = high == col
    far = jnp.abs(high - col)
    top = nc - 1
    above = (jnp.minimum(high + 1, top) * ratio + low, col)
    below = (jnp.maximum(high - 1, 0) * ratio + low, col)
    goes_up = jnp.logical_and(high >= col, high < top)
    goes_down = jnp.logical_and(high <= col, high > 0)

    def onward(where, src, e):
        dst = xc_ref.at[low, where]
        up = pltpu.make_async_remote_copy(
            src_ref=src, dst_ref=dst, send_sem=send_sem.at[up_sem], recv_sem=recv_sem.at[chain_base + e],
            device_id=above, device_id_type=MESH,
        )
        down = pltpu.make_async_remote_copy(
            src_ref=src, dst_ref=dst, send_sem=send_sem.at[down_sem], recv_sem=recv_sem.at[chain_base + e],
            device_id=below, device_id_type=MESH,
        )
        sibs = [remote(src, dst, sib_base + q - 1, low_peer(q)) for q in range(1, ratio)]
        return up, down, sibs

    def links(e, src_is_own):
        d, h = order[e]
        where = own_rows(h, lax.rem(col - d + nc, nc))
        src = xr_ref.at[where] if src_is_own else xc_ref.at[low, where]
        return (where,) + onward(where, src, e)

    def send_on(e, up, down, sibs):
        owner = lax.rem(col - order[e][0] + nc, nc)

        @pl.when(jnp.logical_and(goes_up, owner != top))
        def _():
            up.start()

        @pl.when(jnp.logical_and(goes_down, owner != 0))
        def _():
            down.start()

        for sib in sibs:
            sib.start()

    def keep(e):
        d, h = order[e]
        where = own_rows(h, lax.rem(col - d + nc, nc))
        return pltpu.make_async_copy(xr_ref.at[where], xc_ref.at[low, where], keep_sem.at[0])

    def relay_source(e):
        d, h = order[e]
        where, up, down, sibs = links(e, True)
        send_on(e, up, down, sibs)
        keep(e).start()

    def relay(e):
        where, up, down, sibs = links(e, False)
        up.wait_recv()
        send_on(e, up, down, sibs)

    side_recv = chain_base + pieces
    side_send = take(2 * nc)
    last_up = jnp.logical_and(col == top, high < top)
    last_down = jnp.logical_and(col == 0, high > 0)

    def side(src, slot, h, lag, device):
        dst = side_ref.at[slot, pl.ds(h * sub, sub)]
        return pltpu.make_async_remote_copy(
            src_ref=src, dst_ref=dst, send_sem=send_sem.at[side_send + lag],
            recv_sem=recv_sem.at[side_recv + slot * parts + h], device_id=device, device_id_type=MESH,
        )

    def deliver(slot, h, lag, upward):
        first = (h // 2) * 2 * nc + 2 + (h % 2) * (nc - 1)
        e = first + (slot if upward else slot - 1)
        return pltpu.make_async_remote_copy(
            src_ref=side_ref.at[slot, pl.ds(h * sub, sub)], dst_ref=xc_ref.at[low, own_rows(h, top if upward else 0)],
            send_sem=send_sem.at[side_send + nc + lag], recv_sem=recv_sem.at[chain_base + e],
            device_id=(row, slot), device_id_type=MESH,
        )

    def side_start(h):
        for test, device in ((last_up, above), (last_down, below)):
            @pl.when(test)
            def _():
                side(xr_ref.at[own_rows(h, col)], high, h, 0, device).start()

    def side_edges(lag):
        up, down = high - lag, high + lag
        return (
            (True, up, jnp.logical_and(col == top, up >= 0), above, high < top),
            (False, down, jnp.logical_and(col == 0, down <= top), below, high > 0),
        )

    def side_forward(h, lag):
        for _, slot, edge, device, onward_too in side_edges(lag):
            @pl.when(edge)
            def _():
                copy = side(side_ref.at[slot, pl.ds(h * sub, sub)], slot, h, lag, device)
                copy.wait_recv()
                pl.when(onward_too)(copy.start)

    def side_deliver(h, lag):
        for upward, slot, edge, _, _ in side_edges(lag):
            pl.when(edge)(deliver(slot, h, lag, upward).start)

    def each_lag(act, h, lag):
        for each in range(lag, nc if lag == 3 else min(lag + 1, nc)):
            act(h, each)

    def side_take(h):
        @pl.when(jnp.logical_not(source))
        def _():
            e = (h // 2) * 2 * nc + 2 + (h % 2) * (nc - 1) + jnp.where(high > col, col, col - 1)
            where = own_rows(h, jnp.where(high > col, top, 0))
            up, _, sibs = onward(where, xc_ref.at[low, where], e)
            up.wait_recv()
            for sib in sibs:
                sib.start()

    def side_drain():
        span = pl.ds(0, parts * sub)
        for upward in (True, False):
            for lag in range(nc):
                slot = high - lag if upward else high + lag
                edge = jnp.logical_and(col == top, slot >= 0) if upward else jnp.logical_and(col == 0, slot <= top)
                whole = pltpu.make_async_remote_copy(
                    src_ref=tland.at[span], dst_ref=tland.at[span], send_sem=send_sem.at[side_send + lag],
                    recv_sem=recv_sem.at[side_recv], device_id=above, device_id_type=MESH,
                )
                pl.when(jnp.logical_and(edge, high < top if upward else high > 0))(whole.wait_send)
                if lag > 0:
                    whole = pltpu.make_async_remote_copy(
                        src_ref=tland.at[span], dst_ref=tland.at[span], send_sem=send_sem.at[side_send + nc + lag],
                        recv_sem=recv_sem.at[side_recv], device_id=above, device_id_type=MESH,
                    )
                    pl.when(edge)(whole.wait_send)

    def emit(pieces_now):
        @pl.when(source)
        def _():
            for e in pieces_now:
                relay_source(e)

    def group(h):
        return [e for e in range(pieces) if order[e][1] == h and order[e][0] > 0]

    def own(h):
        return [order.index((0, h))]

    def point(k):
        for test, lag in ((far == 1, 0), (far == 2, 2), (far > 2, 4)):
            if 0 <= k - lag < pieces:
                owner = lax.rem(col - order[k - lag][0] + nc, nc)
                chained = owner != jnp.where(high > col, top, 0)
                pl.when(jnp.logical_and(test, chained))(functools.partial(relay, k - lag))

    for h in range(parts):
        loads[h].wait()
        where = slice(h * part, (h + 1) * part)
        a, b = split(block[where, :])
        t_ref[where, :] = matmul(a, high_op[...]) + matmul(a, low_op[...]) + matmul(b, high_op[...])
        if h == 0:
            pl.semaphore_wait(barrier, ratio - 1 + 2 * (nc - 1))
        if h < 2:
            scatter(h)
        if h == parts - 2:
            operator(row * rows, rows, store_row)

    def reduced(acc, full, land, spread):
        start, length, slot = 0, acc.shape[0], 0
        spots = []

        def exchange_all(level, pairs, count):
            n, me, peer = levels[level]
            base = take(1)
            for d in range(1, n):
                src, dst = pairs(d)
                remote(src, dst, base, peer(d)).start()
            every = land.at[pl.ds(0, (n - 1) * count)]
            return remote(every, every, base, peer(1))

        for level, (n, me, peer) in enumerate(levels):
            whole = level == 2 and not spread
            segment = length if whole else length // n

            def scattered(d):
                begin = start if whole else pl.multiple_of(start + lax.rem(me + d, n) * segment, 8)
                return acc.at[pl.ds(begin, segment)], land.at[pl.ds(slot + (d - 1) * segment, segment)]

            end = exchange_all(level, scattered, segment)
            yield
            if not whole:
                start = pl.multiple_of(start + me * segment, 8)
                spots.append((start, segment))
            length = segment
            end.wait()
            where = pl.ds(start, length)
            mine = acc[where, :]
            for d in range(1, n):
                mine = mine + land[pl.ds(slot + (d - 1) * segment, segment), :]
            slot += (n - 1) * segment
            if level == 2:
                full[where, :] = mine
            else:
                acc[where, :] = mine
        for level in (2, 1, 0) if spread else (1, 0):
            begin, segment = spots[level]
            where = full.at[pl.ds(begin, segment)]
            end = exchange_all(level, lambda d: (where, where), segment)
            yield
            end.wait()
        yield

    def sums(i):
        return lax.dot_general(
            row_op[:, i * BLK : (i + 1) * BLK], t_ref[:, : (i + 1) * BLK], (((0,), (0,)), ((), ())),
            precision=MID, preferred_element_type=jnp.float32,
        )

    first = reduced(acc0, full0, land0, False)
    rest = reduced(acc1, full1, land1, True)
    place = 0
    settle(0)
    for i in range(size // BLK):
        blocks = sums(i)
        if i == 0:
            acc0[:BLK, :] = blocks
            if acc0.shape[0] > BLK:
                acc0[BLK:, :] = jnp.zeros((acc0.shape[0] - BLK, BLK), jnp.float32)
            next(first)
            continue
        for j in range(i + 1):
            acc1[place : place + BLK, :] = blocks[:, j * BLK : (j + 1) * BLK]
            place += BLK
        if i == 1:
            next(first)
            settle(1)
        if i == 2:
            spread(0)
            next(first)
            emit(own(0))
            side_start(0)
    predicted = jnp.zeros((1, size), jnp.float32)
    for q in range(rows // width):
        state = pack_ref[state_row + q : state_row + q + 1, :]
        predicted = predicted + jnp.dot(
            state, row_op[q * width : (q + 1) * width, :], precision=HI, preferred_element_type=jnp.float32
        )
    predicted = jnp.where(col == 0, predicted, 0.0)
    acc1[place:, :] = jnp.zeros((acc1.shape[0] - place, BLK), jnp.float32)
    for i in range(size // BLK):
        acc1[place + i : place + i + 1, :] = predicted[:, i * BLK : (i + 1) * BLK]
    next(rest)
    spread(1)
    side_start(1)
    pass_on(0)
    emit(own(1))
    next(first)
    next(rest)
    pass_on(1)
    next(first)
    point(0)
    next(first)
    next(rest)
    arrive(0)
    emit(group(0)[:1])
    if parts > 2:
        scatter(2)
        scatter(3)
    point(1)

    same = lax.broadcasted_iota(jnp.int32, (BLK, BLK), 0) == lax.broadcasted_iota(jnp.int32, (BLK, BLK), 1)

    def place_block(i, j, square):
        if i == j:
            lane = i * BLK % width
            line = var_row + i * BLK // width
            diagonal = pack_ref[line : line + 1, lane : lane + BLK]
            square = 0.5 * (square + square.T) + jnp.where(same, diagonal, 0.0)
        mat[i * BLK : (i + 1) * BLK, j * BLK : (j + 1) * BLK] = square
        if i != j:
            mat[j * BLK : (j + 1) * BLK, i * BLK : (i + 1) * BLK] = square.T

    place_block(0, 0, full0[:BLK, :])
    mat[:, size:] = jnp.zeros((size, size), jnp.float32)

    points = {2: 2, 4: 6, 5: 7, 6: 8, 7: 9, 8: 10, 10: 11, 11: 12, 12: 13, 13: 14, 15: 15}

    sides = {
        4: [(side_forward, 0, 2), (side_forward, 1, 2)],
        6: [(side_forward, 2, 1), (side_deliver, 0, 1), (side_deliver, 1, 1)],
        7: [(side_forward, 3, 1)],
        8: [(side_deliver, 0, 2), (side_deliver, 1, 2), (side_forward, 0, 3), (side_forward, 1, 3), (side_deliver, 0, 3), (side_deliver, 1, 3)],
        9: [(side_forward, 2, 2), (side_deliver, 2, 1), (side_deliver, 3, 1)],
        11: [(side_forward, 3, 2)],
        12: [(side_deliver, 2, 2), (side_deliver, 3, 2), (side_forward, 2, 3), (side_deliver, 2, 3)],
        14: [(side_forward, 3, 3), (side_deliver, 3, 3)],
    }

    def hook(slot):
        if slot == 1:
            next(rest)
            emit(group(0)[1:])
            for h in range(2):
                each_lag(side_forward, h, 1)
        if parts > 2 and slot == 2:
            settle(2)
        if slot == 3:
            next(rest)
            arrive(1)
            emit(group(1))
        if parts > 2:
            if slot == 3:
                settle(3)
            if slot == 4:
                pass_on(2)
            if slot == 5:
                pass_on(3)
            if slot == 7:
                arrive(2)
                emit(group(2))
            if slot == 9:
                arrive(3)
                emit(group(3))
        for act, h, lag in sides.get(slot, ()):
            if h < parts:
                each_lag(act, h, lag)
        if slot in points:
            point(points[slot])

    def ready(b):
        if b == 0:
            point(3)
            if parts > 2:
                spread(2)
                side_start(2)
                emit(own(2))
            next(rest)
            if parts > 2:
                spread(3)
                side_start(3)
                emit(own(3))
            point(4)
            next(rest)
            point(5)
            for index, (i, j) in enumerate(pair_blocks(size)[1:]):
                place_block(i, j, full1[index * BLK : (index + 1) * BLK, :])
            innov_ref[...] = jnp.zeros((8, BLK), jnp.float32)
            for i in range(size // BLK):
                lane = i * BLK % width
                line = value_row + i * BLK // width
                value = pack_ref[line : line + 1, lane : lane + BLK]
                innov_ref[i : i + 1, :] = value - full1[place + i : place + i + 1, :]

    factor_inverse(mat, work, hook, ready)
    done = [16]

    def advance(last):
        while done[0] <= last:
            point(done[0])
            done[0] += 1

    advance(16)
    middle = size // 2
    across, along = (((1,), (1,)), ((), ())), (((1,), (0,)), ((), ()))
    high_w, low_w = split(mat[:, size:])

    def product(value, rows_w, lanes_w, dims):
        a, b = split(value)
        c, d = high_w[rows_w, lanes_w], low_w[rows_w, lanes_w]
        return matmul(a, c, dims) + matmul(a, d, dims) + matmul(b, c, dims)

    lower, upper, every = slice(0, middle), slice(middle, size), slice(0, size)
    step = rows // UNITS
    results = []
    for c in range(UNITS):
        where = slice(c * step, (c + 1) * step)
        gain_left = product(xr_ref[where, lower], lower, lower, across)
        gain_right = product(xr_ref[where, :], upper, every, across)
        u_ref[where, lower] = product(jnp.concatenate([gain_left, gain_right], axis=1), every, lower, along)
        u_ref[where, upper] = product(gain_right, upper, upper, along)
        results.append(pltpu.make_async_copy(u_ref.at[pl.ds(c * step, step)], u_out.at[pl.ds(c * step, step)], keep_sem.at[1]))
        results[-1].start()
        advance(done[0])
    for h in range(parts):
        side_take(h)
    advance(pieces + 3)
    pltpu.make_async_copy(u_ref, u_out, keep_sem.at[1]).wait()
    everything = pl.ds(0, rows)

    @pl.when(source)
    def _():
        pltpu.make_async_copy(xr_ref, xc_ref.at[low], keep_sem.at[0]).wait()

    for h in range(parts):
        plane[h][1][3].wait_send()
    _, _, sibs = onward(everything, xr_ref, 0)
    fewer = pl.ds(0, rows - rows // nc)
    up, down, _ = onward(fewer, xr_ref.at[fewer], 0)

    @pl.when(goes_up)
    def _():
        up.wait_send()

    @pl.when(goes_down)
    def _():
        down.wait_send()

    for sib in sibs:
        sib.wait()
    side_drain()


def padded(count, unit):
    return -(-count // unit) * unit


def exchange(mesh, covariance, pack, batches, foot):
    nr, nc = mesh.shape["row"], mesh.shape["col"]
    ratio = nr // nc
    rows, cols = covariance.shape
    size = batches * pack.shape[1]
    parts = part_count(rows, nc)
    group = ratio * nc
    lead = padded(BLK, 8 * group)
    follow = padded((len(pair_blocks(size)) - 1) * BLK + 8, 8 * group * nc)
    half, quarter = follow // ratio, follow // group
    land0 = (ratio - 1) * (lead // ratio) + 2 * (nc - 1) * (lead // group)
    land1 = (ratio - 1) * half + (nc - 1) * quarter + (nc - 1) * (quarter // nc)
    tall, flat = plane_shape(nc)
    sub = rows // (parts * nc)
    pieces = nc * parts
    sends = 2 * 2 * 3 - 1 + 4 * parts + ratio + 1 + 2 * nc
    receives = sends + pieces + nc * parts
    f32 = jnp.float32
    vmem = pl.BlockSpec(memory_space=pltpu.VMEM)
    return pl.pallas_call(
        functools.partial(kernel, nr, nc, parts, batches, foot),
        out_shape=(
            jax.ShapeDtypeStruct((rows, size), f32),
            jax.ShapeDtypeStruct((ratio, rows, size), f32),
            jax.ShapeDtypeStruct((8, BLK), f32),
        ),
        in_specs=[pl.BlockSpec(memory_space=pl.ANY), vmem],
        out_specs=(pl.BlockSpec(memory_space=pl.ANY),) * 2 + (vmem,),
        scratch_shapes=[
            pltpu.VMEM((rows, size), f32),
            pltpu.SemaphoreType.DMA((2,)),
            pltpu.VMEM((rows, cols), f32),
            pltpu.VMEM((cols, size), jnp.bfloat16),
            pltpu.VMEM((cols, size), jnp.bfloat16),
            pltpu.VMEM((rows, size), f32),
            pltpu.VMEM((rows, size), f32),
            pltpu.VMEM((rows, size), f32),
            pltpu.VMEM((lead, BLK), f32),
            pltpu.VMEM((lead, BLK), f32),
            pltpu.VMEM((land0, BLK), f32),
            pltpu.VMEM((follow, BLK), f32),
            pltpu.VMEM((follow, BLK), f32),
            pltpu.VMEM((land1, BLK), f32),
            pltpu.VMEM((nc, parts * sub, size), f32),
            pltpu.VMEM((max((flat - 1) * tall, parts) * sub, size), f32),
            pltpu.VMEM((parts, flat - 1, tall, sub, size // 2), f32),
            pltpu.VMEM((parts, tall - 1, flat, sub, size // 2), f32),
            pltpu.VMEM((parts, tall, sub, size // 2), f32),
            pltpu.VMEM((parts, flat, sub, size // 2), f32),
            pltpu.VMEM((parts, tall - 1, sub, size // 2), f32),
            pltpu.VMEM((parts, flat - 1, sub, size // 2), f32),
            pltpu.VMEM((size, 2 * size), f32),
            pltpu.VMEM((BLK, 2 * BLK), f32),
            pltpu.SemaphoreType.DMA((sends,)),
            pltpu.SemaphoreType.DMA((receives,)),
            pltpu.SemaphoreType.DMA((parts,)),
        ],
        compiler_params=pltpu.CompilerParams(collective_id=0, has_side_effects=True, vmem_limit_bytes=40 * 1024 * 1024),
    )(covariance, pack)


def on_device(mesh, covariance, state_mean, obs_values, obs_cells, obs_weights, obs_variance):
    rows_dev, cols_dev = covariance.shape
    batches, foot, width = obs_cells.shape
    total = batches * width
    pack = jnp.concatenate(
        [
            obs_cells.astype(jnp.float32).reshape(batches * foot, width),
            obs_weights.reshape(batches * foot, width),
            obs_variance,
            obs_values,
            state_mean.reshape(rows_dev // width, width),
        ],
        axis=0,
    )
    u, cross_cols, innov = exchange(mesh, covariance, pack, batches, foot)
    innov = innov[: total // BLK].reshape(total)
    mean = state_mean + jnp.sum(u * innov[None, :], axis=1)
    update = jnp.dot(u, cross_cols.reshape(cols_dev, total).T, precision=MID, preferred_element_type=jnp.float32)
    return (covariance - update, mean)


def solution(mesh):
    return jax.shard_map(
        functools.partial(on_device, mesh),
        mesh=mesh,
        in_specs=(P("row", "col"), P("row"), P(), P(), P(), P()),
        out_specs=(P("row", "col"), P("row")),
        check_vma=False,
    )
```
